32 devices in a mesh: dp: 2 (over x), tok: 4 (over z), mp: 4 (over y, core).
Axes of the slice: x: 2, y: 2, z: 4, core: 2. Of those that a mesh axis runs over, the one named last changes fastest.
Arguments:
- tokens: bfloat16 [16384, 1024], P(('dp', 'tok'), 'mp'), may hold values from -6 to 6
- in_weight: bfloat16 [1024, 3, 1024], P(('dp', 'tok'), None, 'mp'), may hold values from -0.1875 to 0.1875
- conv_kernel: bfloat16 [3, 1024], P(None, 'mp'), may hold values from -2.5 to 2.5
- out_weight: bfloat16 [1024, 1024], P('mp', ('dp', 'tok')), may hold values from -0.1875 to 0.1875
- gate_weight: bfloat16 [1024, 4608], P(('dp', 'tok'), 'mp'), may hold values from -0.1875 to 0.1875
- up_weight: bfloat16 [1024, 4608], P(('dp', 'tok'), 'mp'), may hold values from -0.1875 to 0.1875
- down_weight: bfloat16 [4608, 1024], P('mp', ('dp', 'tok')), may hold values from -0.09375 to 0.09375
- mixer_norm_gain: float32 [1024], replicated, may hold values from 0.5 to 1.5
- gain_ffn: float32 [1024], replicated, may hold values from 0.5 to 1.5
- cotangent: bfloat16 [16384, 1024], P(('dp', 'tok'), 'mp'), may hold values from -6 to 6
Outputs:
- mixed: bfloat16 [16384, 1024], P(('dp', 'tok'), 'mp')
- input_token_gradient: float32 [16384, 1024], P(('dp', 'tok'), 'mp')
- grad_in_weight: float32 [1024, 3, 1024], P(('dp', 'tok'), None, 'mp')
- grad_conv_kernel: float32 [3, 1024], P(None, 'mp')
- grad_out_weight: float32 [1024, 1024], P('mp', ('dp', 'tok'))
- grad_gate_weight: float32 [1024, 4608], P(('dp', 'tok'), 'mp')
- grad_up_weight: float32 [1024, 4608], P(('dp', 'tok'), 'mp')
- grad_down_weight: float32 [4608, 1024], P('mp', ('dp', 'tok'))
- grad_gain_mix: float32 [1024], P('mp')
- grad_gain_ffn: float32 [1024], P('mp')
The draws below stay inside these ranges and needn't reach their ends.
All inputs are finite; a program needn't handle non-finite values.
Results may differ from the reference program's by a relative error of at most 0.011.
Values may be sent and summed in bfloat16 or wider, within the bound.
No kernel may reach another device: no remote copies, remote signals or barrier semaphores. Data moves between devices by JAX's collectives and lax.ppermute only.
A program may use at most 192 MiB of HBM per device.

```python
import jax
import jax.numpy as jnp
from jax import lax

D = 1024
FF = 4608
CONV = 3
SEQ = 8192
TOKENS = 16384


def with_spikes(drawn, key, source, target, shards_of, factor):
    def block_of(position):
        return (jnp.arange(drawn.shape[position]) // (drawn.shape[position] // shards_of)).reshape((-1,) + (1,) * (drawn.ndim - 1 - position))

    first = jax.random.permutation(key, shards_of)[block_of(target)]
    second = (block_of(target) + shards_of // 2) % shards_of
    return jnp.where((block_of(source) == first) | (block_of(source) == second), factor * drawn, drawn)


def block_scale(key, dims, shards, smallest, largest):
    def one(position, shards_of):
        steps = jax.random.uniform(jax.random.fold_in(jax.random.fold_in(key, 6), position), (shards_of,), jnp.float32, smallest / len(shards), largest / len(shards))
        return jnp.repeat(jnp.exp(steps), dims[position] // shards_of).reshape((-1,) + (1,) * (len(dims) - position - 1))

    gain = one(*shards[0])
    for cut in shards[1:]:
        gain = gain * one(*cut)
    return gain


def normal_values(own_key, dims, spread, limit, cuts=(), held_as=jnp.bfloat16):
    values = spread * jax.random.normal(own_key, dims, jnp.float32)
    if cuts:
        values = values * block_scale(own_key, dims, cuts, -0.22, 0.18)
    return jnp.clip(values, -limit, limit).astype(held_as)


def noise_with(own_key, dims, deviation, most, shards, heavy, held_as=jnp.bfloat16):
    entries = deviation * jax.random.normal(own_key, dims, jnp.float32)
    if shards:
        entries = entries * block_scale(own_key, dims, shards, -0.22, 0.18)
    return jnp.clip(with_spikes(entries, jax.random.fold_in(own_key, 3), *heavy), -most, most).astype(held_as)


def setup_inputs(seed: int = 0) -> dict:
    streams_of = jax.random.split(jax.random.key(seed), 11)
    tokens = normal_values(streams_of[0], (TOKENS, D), 1.0, 6.0, ((0, 8), (1, 4)))
    in_weight = normal_values(streams_of[1], (D, CONV, D), D ** -0.5, 0.1875, ((0, 8), (2, 4)))
    conv_kernel = normal_values(streams_of[2], (CONV, D), 0.6, 2.5, ((1, 4),))
    out_weight = normal_values(streams_of[3], (D, D), D ** -0.5, 0.1875, ((0, 4), (1, 8)))
    gate_weight = normal_values(streams_of[4], (D, FF), D ** -0.5, 0.1875, ((0, 8), (1, 4)))
    up_weight = normal_values(streams_of[5], (D, FF), D ** -0.5, 0.1875, ((0, 8), (1, 4)))
    down_weight = normal_values(streams_of[6], (FF, D), FF ** -0.5, 0.09375, ((0, 4), (1, 8)))
    mixer_norm_gain = jnp.clip(1.0 + 0.1 * jax.random.normal(streams_of[7], (D,), jnp.float32), 0.5, 1.5)
    gain_ffn = jnp.clip(1.0 + 0.1 * jax.random.normal(streams_of[8], (D,), jnp.float32), 0.5, 1.5)
    cotangent = noise_with(streams_of[9], (TOKENS, D), 1.0, 6.0, ((0, 8), (1, 4)), (0, 1, 8, 2.0))
    return dict(tokens=tokens, in_weight=in_weight, conv_kernel=conv_kernel, out_weight=out_weight, gate_weight=gate_weight, up_weight=up_weight, down_weight=down_weight, mixer_norm_gain=mixer_norm_gain, gain_ffn=gain_ffn, cotangent=cotangent)


eps_norm = 1e-05

@jax.custom_vjp
def low(v):
    return lax.optimization_barrier(v.astype(jnp.bfloat16)).astype(jnp.float32)

@jax.custom_vjp
def low_back(v):
    return v

def low_keep(v):
    return (low(v), None)

def low_pass(kept, grad):
    return (grad,)

def back_keep(v):
    return (v, None)

def back_low(kept, grad):
    return (low(grad),)
low.defvjp(low_keep, low_pass)
low_back.defvjp(back_keep, back_low)

def matmul(left, right):
    return jnp.dot(left, right, precision=lax.Precision.HIGHEST)

def block(inputs, in_weight, conv_kernel, out_weight, gate_weight, up_weight, down_weight, mixer_norm_gain, gain_ffn):
    mixer_inverse_norm = lax.rsqrt(lax.optimization_barrier(jnp.mean(inputs * inputs, -1, keepdims=True)) + eps_norm)
    mixer_hidden = low(inputs * mixer_inverse_norm * mixer_norm_gain)
    proj = low_back(jnp.einsum('td,dkc->tkc', mixer_hidden, in_weight, precision=lax.Precision.HIGHEST))
    gated = low(proj[:, 0] * proj[:, 2])
    padded = jnp.concatenate([jnp.zeros((2, gated.shape[1]), jnp.float32), gated], 0)
    conv = low_back(conv_kernel[0] * padded[:-2] + conv_kernel[1] * padded[1:-1] + conv_kernel[2] * padded[2:])
    mixed_in = low(proj[:, 1] * conv)
    mix_out = low_back(matmul(mixed_in, out_weight))
    residual_stream = inputs + mix_out
    feedforward_inverse_norm = lax.rsqrt(lax.optimization_barrier(jnp.mean(residual_stream * residual_stream, -1, keepdims=True)) + eps_norm)
    feedforward_hidden = low(residual_stream * feedforward_inverse_norm * gain_ffn)
    gate = low_back(matmul(feedforward_hidden, gate_weight))
    upper = low_back(matmul(feedforward_hidden, up_weight))
    hidden = low(jax.nn.silu(gate) * upper)
    return residual_stream + matmul(hidden, down_weight)

def reference(tokens, in_weight, conv_kernel, out_weight, gate_weight, up_weight, down_weight, mixer_norm_gain, gain_ffn, cotangent):
    params = (in_weight.astype(jnp.float32), conv_kernel.astype(jnp.float32), out_weight.astype(jnp.float32), gate_weight.astype(jnp.float32), up_weight.astype(jnp.float32), down_weight.astype(jnp.float32), mixer_norm_gain.astype(jnp.float32), gain_ffn.astype(jnp.float32))
    sequence_count = TOKENS // SEQ
    inputs = tokens.astype(jnp.float32).reshape(sequence_count, SEQ, D)
    cots = cotangent.astype(jnp.float32).reshape(sequence_count, SEQ, D)

    def one_seq(totals, pair):
        seq_in, seq_cot = pair
        result, pull = jax.vjp(block, seq_in, *params)
        grads = pull(seq_cot)
        totals = tuple((a + b for a, b in zip(totals, grads[1:])))
        return (totals, (result, grads[0]))
    start = tuple((jnp.zeros(p.shape, jnp.float32) for p in params))
    totals, (outputs, grad_in) = lax.scan(one_seq, start, (inputs, cots))
    return (outputs.reshape(TOKENS, D).astype(jnp.bfloat16), grad_in.reshape(TOKENS, D), totals[0], totals[1], totals[2], totals[3], totals[4], totals[5], totals[6], totals[7])
```

```python
import jax
import jax.numpy as jnp
from jax import lax
from jax.sharding import Mesh
from jax.sharding import PartitionSpec as P

EPS = 1e-05
F32 = jnp.float32
BF16 = jnp.bfloat16


def swap(value, axis):
    return lax.ppermute(value, axis, [(0, 1), (1, 0)])


def fetch(value, axis, distance):
    size = lax.axis_size(axis)
    return lax.ppermute(value, axis, [(s, (s - distance) % size) for s in range(size)])


def deliver(value, axis, distance):
    size = lax.axis_size(axis)
    return lax.ppermute(value, axis, [(s, (s + distance) % size) for s in range(size)])


def dot(left, right, contract):
    return lax.dot_general(left, right, (contract, ((), ())), preferred_element_type=F32)


def nn(left, right):
    return dot(left, right, ((1,), (0,)))


def nt(left, right):
    return dot(left, right, ((1,), (1,)))


def tn(left, right):
    return dot(left, right, ((0,), (0,)))


def total(values):
    result = values[0].astype(F32)
    for value in values[1:]:
        result = result + value.astype(F32)
    return result


def gather_rows(shard):
    blocks = [shard] + [fetch(shard, "tok", j) for j in range(1, lax.axis_size("tok"))]
    parts = list(blocks)
    for i in range(1, lax.axis_size("dp")):
        parts += [fetch(block, "dp", i) for block in blocks]
    own = jnp.concatenate(parts, 0)
    return blocks[-1], own, swap(own, "c")


def scatter_rows(own, other):
    pair = total([own, swap(other, "c")]).astype(BF16)
    steps = lax.axis_size("dp")
    size = pair.shape[0] // steps
    mine = total(
        [pair[:size]]
        + [deliver(pair[i * size : (i + 1) * size], "dp", i) for i in range(1, steps)]
    ).astype(BF16)
    steps = lax.axis_size("tok")
    size = mine.shape[0] // steps
    return total(
        [mine[:size]]
        + [deliver(mine[i * size : (i + 1) * size], "tok", i) for i in range(1, steps)]
    )


def body(
    tokens,
    in_weight,
    conv_kernel,
    out_weight,
    gate_weight,
    up_weight,
    down_weight,
    mixer_norm_gain,
    gain_ffn,
    cotangent,
):
    x, z, y, c = (lax.axis_index(name) for name in ("dp", "tok", "y", "c"))
    nx, nz = lax.axis_size("dp"), lax.axis_size("tok")
    width = tokens.shape[1]
    features = 4 * width
    rows = tokens.shape[0] // 2
    half = rows // 2
    chunk = in_weight.shape[0]

    position = lax.broadcasted_iota(jnp.int32, (features, features), 1)
    block = position // chunk
    spread = (((x + block // nz) % nx) * nz + (z + block % nz) % nz) * chunk + position % chunk
    place = lax.broadcasted_iota(jnp.int32, (features, features), 0)
    piece = place // width
    natural = (2 * (y ^ (piece // 2)) + (c ^ (piece % 2))) * width + place % width
    order = (natural == spread).astype(BF16)

    def spread_gain(gain):
        return jnp.sum(jnp.where(place == spread, gain[:, None], 0.0), 0)

    def pick_rows(value, index, size):
        return lax.dynamic_slice_in_dim(value, index * size, size, 0)

    def feature_rows(value):
        mine, theirs = pick_rows(value, c, rows), pick_rows(value, 1 - c, rows)
        return jnp.concatenate([mine, swap(theirs, "c")], 1)

    def by_rank(index, first, second):
        return jnp.where(
            index == 0,
            jnp.concatenate([first, second], 0),
            jnp.concatenate([second, first], 0),
        )

    near = feature_rows(tokens)
    full = nn(jnp.concatenate([near, swap(near, "y")], 1), order).astype(BF16)

    flat_in = in_weight.reshape(chunk, 3 * width)
    first = jnp.concatenate([flat_in, out_weight.T], 1)
    last, first_own, first_other = gather_rows(first)
    gate_weight, up_weight, down_rows, last = lax.optimization_barrier(
        (gate_weight, up_weight, down_weight.T, last)
    )
    last, gate_own, gate_other = gather_rows(gate_weight)
    up_weight, down_rows, last = lax.optimization_barrier((up_weight, down_rows, last))
    last, up_own, up_other = gather_rows(up_weight)
    down_rows, last = lax.optimization_barrier((down_rows, last))
    last, down_own, down_other = gather_rows(down_rows)
    w_in = (first_own[:, : 3 * width], first_other[:, : 3 * width])
    w_out = (first_own[:, 3 * width :], first_other[:, 3 * width :])
    w_gate, w_up, w_down = (gate_own, gate_other), (up_own, up_other), (down_own, down_other)

    near_cot = feature_rows(cotangent)
    pieces_cot = jnp.concatenate([near_cot, swap(near_cot, "y")], 1)
    pieces_cot = jnp.concatenate(
        [pick_rows(pieces_cot, y, half), pick_rows(pieces_cot, 1 - y, half)], 0
    )
    cot = nn(pieces_cot, order).astype(BF16)

    full32 = full.astype(F32)
    inverse_mix = lax.rsqrt(jnp.mean(full32 * full32, -1, keepdims=True) + EPS)
    gain_mix_spread = spread_gain(mixer_norm_gain)
    gain_ffn_spread = spread_gain(gain_ffn)
    h_mix = (full32 * inverse_mix * gain_mix_spread).astype(BF16)

    def taps_of(which):
        other = swap(conv_kernel, "c")
        return (conv_kernel if which == 0 else other).astype(F32)

    gates = []
    for w in w_in:
        proj = nn(h_mix, w)
        gates.append((proj[:, :width], proj[:, width : 2 * width], proj[:, 2 * width :]))
    gated = [(b * xin).astype(BF16) for b, _, xin in gates]
    ranks = nz * 2
    edge = lax.ppermute(
        jnp.concatenate([gated[1][-2:], gated[0][-2:]], 1),
        ("tok", "c"),
        [(i, i + 1) for i in range(ranks - 1)],
    )
    taps = [taps_of(0), taps_of(1)]
    extended, convs, mixed_in = [], [], []
    for i in range(2):
        ext = jnp.concatenate([edge[:, i * width : (i + 1) * width], gated[i]], 0).astype(F32)
        conv = taps[i][0] * ext[:rows] + taps[i][1] * ext[1 : rows + 1] + taps[i][2] * ext[2:]
        extended.append(ext)
        convs.append(conv)
        mixed_in.append((gates[i][1] * conv).astype(BF16))

    def project_out(index):
        return nt(pick_rows(mixed_in[0], index, half), w_out[0]) + nt(
            pick_rows(mixed_in[1], index, half), w_out[1]
        )

    arrived = swap(project_out(1 - y).astype(BF16), "y")
    residual = pick_rows(full, y, half).astype(F32) + project_out(y) + arrived.astype(F32)

    inverse_ffn = lax.rsqrt(jnp.mean(residual * residual, -1, keepdims=True) + EPS)
    normalized = residual * inverse_ffn
    h_own = (normalized * gain_ffn_spread).astype(BF16)
    h = jnp.concatenate([h_own, swap(h_own, "y")], 0)
    hidden, d_gate, d_up = [], [], []
    for i in range(2):
        gate, up = nn(h, w_gate[i]), nn(h, w_up[i])
        sigma = jax.nn.sigmoid(gate)
        silu = gate * sigma
        hidden.append((silu * up).astype(BF16))
        dhid = nn(cot, w_down[i])
        d_gate.append((dhid * up * sigma * (1.0 + gate * (1.0 - sigma))).astype(BF16))
        d_up.append((dhid * silu).astype(BF16))

    def back(part):
        return sum(
            nt(d_gate[i][part], w_gate[i]) + nt(d_up[i][part], w_up[i]) for i in range(2)
        )

    arrived = swap(back(slice(half, None)).astype(BF16), "y")
    d_h = back(slice(0, half)) + arrived.astype(F32)
    grad_gain_ffn = jnp.sum(d_h * normalized, 0)
    scaled = d_h * gain_ffn_spread
    d_res = cot[:half].astype(F32) + inverse_ffn * (
        scaled - normalized * jnp.mean(scaled * normalized, -1, keepdims=True)
    )
    d_res_own = d_res.astype(BF16)
    d_res_full = by_rank(y, d_res_own, swap(d_res_own, "y"))

    grad_down = scatter_rows(*(tn(cot, hidden[i]).astype(BF16) for i in range(2)))
    grad_gate = scatter_rows(*(tn(h, d_gate[i]).astype(BF16) for i in range(2)))
    grad_up = scatter_rows(*(tn(h, d_up[i]).astype(BF16) for i in range(2)))

    made = nt(hidden[0], w_down[0]) + nt(hidden[1], w_down[1])
    made = jnp.concatenate([made[:half] + residual, made[half:]], 0).astype(BF16)
    made = nt(made, order).astype(BF16)
    arrived = swap(made[:, 2 * width :], "y").astype(F32)
    kept = made[:, : 2 * width].astype(F32)
    out_near = by_rank(
        y,
        (kept[:half] + arrived[half:]).astype(BF16),
        (kept[half:] + arrived[:half]).astype(BF16),
    )
    mixed = by_rank(c, out_near[:, :width], swap(out_near[:, width:], "c"))

    d_conv, d_c = [], []
    for i in range(2):
        d_y = nn(d_res_full, w_out[i])
        d_conv.append((d_y * gates[i][1]).astype(BF16))
        d_c.append(d_y * convs[i])
    after = lax.ppermute(
        jnp.concatenate([d_conv[1][:2], d_conv[0][:2]], 1),
        ("tok", "c"),
        [(i + 1, i) for i in range(ranks - 1)],
    )
    d_proj, grad_taps, row_dot = [], [], 0.0
    for i in range(2):
        ext = jnp.concatenate([d_conv[i], after[:, i * width : (i + 1) * width]], 0).astype(F32)
        mine = ext[:rows]
        grad_taps.append(
            jnp.stack([jnp.sum(mine * extended[i][k : rows + k], 0) for k in range(3)], 0)
        )
        d_gated = taps[i][2] * mine + taps[i][1] * ext[1 : rows + 1] + taps[i][0] * ext[2:]
        b, gate_c, xin = gates[i]
        parts = [(d_gated * xin).astype(BF16), d_c[i].astype(BF16), (d_gated * b).astype(BF16)]
        row_dot = row_dot + jnp.sum(
            parts[0].astype(F32) * b + parts[1].astype(F32) * gate_c + parts[2].astype(F32) * xin,
            -1,
        )
        d_proj.append(jnp.concatenate(parts, 1))
    lanes = 128
    row_dot = row_dot.reshape(rows // lanes, lanes)
    row_mean = ((row_dot + swap(row_dot, "y")) / features).reshape(rows, 1)
    w_in_pieces = [nn(order, w).astype(BF16) for w in w_in]

    def back_in(part):
        return nt(d_proj[0], w_in_pieces[0][part]) + nt(d_proj[1], w_in_pieces[1][part])

    arrived = swap(back_in(slice(2 * width, None)).astype(BF16), "y")
    d_h_mix = back_in(slice(0, 2 * width)) + arrived.astype(F32)
    grad_first = scatter_rows(
        *(
            jnp.concatenate(
                [tn(h_mix, d_proj[i]).astype(BF16), tn(d_res_full, mixed_in[i]).astype(BF16)], 1
            )
            for i in range(2)
        )
    )

    near_normal = near.astype(F32) * inverse_mix
    d_res_near = nt(d_res_full, order[: 2 * width])

    def own_gain(gain):
        return jnp.concatenate(
            [
                lax.dynamic_slice_in_dim(gain, (2 * y + c) * width, width),
                lax.dynamic_slice_in_dim(gain, (2 * y + 1 - c) * width, width),
            ]
        )

    grad_near = d_res_near + inverse_mix * (
        d_h_mix * own_gain(mixer_norm_gain) - near_normal * row_mean
    )
    input_gradient = by_rank(c, grad_near[:, :width], swap(grad_near[:, width:], "c"))

    def place_near(value):
        empty = jnp.zeros((value.shape[0], features), F32)
        empty = lax.dynamic_update_slice(empty, value[:, :width], (0, (2 * y + c) * width))
        return lax.dynamic_update_slice(empty, value[:, width:], (0, (2 * y + 1 - c) * width))

    near_sums = jnp.concatenate(
        [
            jnp.concatenate(grad_taps, 1),
            jnp.sum(d_h_mix * near_normal, 0)[None],
        ],
        0,
    )
    ffn_sum = jnp.sum(jnp.where(place == spread, grad_gain_ffn[None], 0.0), 1)
    sums = lax.psum(
        jnp.concatenate([place_near(near_sums), ffn_sum[None]], 0), ("dp", "tok", "y", "c")
    )
    sums = lax.dynamic_slice_in_dim(sums, (2 * y + c) * width, width, 1)

    return (
        mixed,
        input_gradient,
        grad_first[:, : 3 * width].reshape(chunk, 3, width),
        sums[:3],
        grad_first[:, 3 * width :].T,
        grad_gate,
        grad_up,
        grad_down.T,
        sums[3],
        sums[4],
    )


def solution(mesh):
    split = Mesh(
        mesh.devices.reshape(mesh.shape["dp"], mesh.shape["tok"], mesh.shape["mp"] // 2, 2),
        ("dp", "tok", "y", "c"),
    )
    tok, mp = ("dp", "tok"), ("y", "c")
    return jax.shard_map(
        body,
        mesh=split,
        in_specs=(
            P(tok, mp),
            P(tok, None, mp),
            P(None, mp),
            P(mp, tok),
            P(tok, mp),
            P(tok, mp),
            P(mp, tok),
            P(),
            P(),
            P(tok, mp),
        ),
        out_specs=(
            P(tok, mp),
            P(tok, mp),
            P(tok, None, mp),
            P(None, mp),
            P(mp, tok),
            P(tok, mp),
            P(tok, mp),
            P(mp, tok),
            P(mp),
            P(mp),
        ),
        check_vma=False,
    )
```

```python
import functools

import jax
import jax.numpy as jnp
from jax import lax
from jax.experimental import pallas as pl
from jax.experimental.layout import Layout, with_layout_constraint
from jax.experimental.pallas import tpu as pltpu
from jax.sharding import Mesh
from jax.sharding import PartitionSpec as P

EPS = 1e-05
F32 = jnp.float32
BF16 = jnp.bfloat16
VMEM_LIMIT = 56 * 2**20


def swap(value, axis):
    return lax.ppermute(value, axis, [(0, 1), (1, 0)])


def deliver(value, axis, distance):
    size = lax.axis_size(axis)
    return lax.ppermute(value, axis, [(s, (s + distance) % size) for s in range(size)])


def dot(left, right, contract):
    return lax.dot_general(left, right, (contract, ((), ())), preferred_element_type=F32)


def nn(left, right):
    return dot(left, right, ((1,), (0,)))


def nt(left, right):
    return dot(left, right, ((1,), (1,)))


def tn(left, right):
    return dot(left, right, ((0,), (0,)))


def total(values):
    result = values[0].astype(F32)
    for value in values[1:]:
        result = result + value.astype(F32)
    return result


def tie(*values):
    return lax.optimization_barrier(values)


def pick_rows(value, index, size):
    return lax.dynamic_slice_in_dim(value, index * size, size, 0)


def by_rank(index, first, second, axis=0):
    return jnp.where(
        index == 0,
        jnp.concatenate([first, second], axis),
        jnp.concatenate([second, first], axis),
    )


def for_dp(own, other):
    steps = lax.axis_size("dp")
    size = own.shape[0] // steps
    indices = [(lax.axis_index("dp") + i) % steps for i in range(1, steps)]
    return [
        total([pick_rows(part, index, size) for part in (own, other)]).astype(BF16)
        for index in indices
    ]


def to_dp(pieces):
    return [deliver(piece, "dp", i + 1) for i, piece in enumerate(pieces)]


def to_tok(mine):
    return lax.all_to_all(mine, "tok", split_axis=0, concat_axis=0, tiled=True)


def add_tok(got):
    steps = lax.axis_size("tok")
    size = got.shape[0] // steps
    return total([got[i * size : (i + 1) * size] for i in range(steps)])


def add_dp(own, other, arrived):
    size = arrived[0].shape[0]
    mine = [pick_rows(part, lax.axis_index("dp"), size) for part in (own, other)]
    return total(mine + list(arrived)).astype(BF16)


def sum_over(value, axis):
    size = lax.axis_size(axis)
    if size & (size - 1):
        return lax.psum(value, axis)
    step = 1
    while step < size:
        value = value + lax.ppermute(value, axis, [(s, s ^ step) for s in range(size)])
        step *= 2
    return value


def hidden_kernel(h_own, h_other, cot, w_gate, w_up, w_down, h, hidden, d_gate, d_up):
    features = h.shape[1]
    half = h_own.shape[0]

    @pl.when(pl.program_id(0) == 0)
    def _():
        h[:half, :] = h_own[...]
        h[half:, :] = h_other[...]

    def both(w):
        return jnp.concatenate([w[:, i].reshape(features, w.shape[3]) for i in (0, 1)], 1)

    w_gate, w_up, w_down = both(w_gate), both(w_up), both(w_down)
    width = w_gate.shape[1] // 2
    step = 256
    for start in range(0, h.shape[0], step):
        part = pl.ds(start, step)
        gate, up = nn(h[part, :], w_gate), nn(h[part, :], w_up)
        d_hidden = nn(cot[part, :], w_down)
        sigma = jax.nn.sigmoid(gate)
        silu = gate * sigma
        results = (
            (hidden, silu * up),
            (d_gate, d_hidden * up * sigma * (1.0 + gate * (1.0 - sigma))),
            (d_up, d_hidden * silu),
        )
        for ref, value in results:
            value = value.astype(BF16)
            ref[0, part, :] = value[:, :width]
            ref[1, part, :] = value[:, width:]


def hidden_units(h_own, h_other, cot, weights):
    rows, features = cot.shape
    blocks, _, chunk, width = weights.shape
    width //= 3
    tile = 128
    tiles = width // tile

    def of(matrix):
        return pl.BlockSpec((blocks, 2, chunk, tile), lambda j: (0, 0, 0, matrix * tiles + j))

    whole = pl.BlockSpec((rows, features), lambda j: (0, 0))
    half = pl.BlockSpec((rows // 2, features), lambda j: (0, 0))
    return pl.pallas_call(
        hidden_kernel,
        out_shape=[jax.ShapeDtypeStruct((rows, features), BF16)]
        + [jax.ShapeDtypeStruct((2, rows, width), BF16)] * 3,
        grid=(tiles,),
        in_specs=[half, half, whole, of(0), of(1), of(2)],
        out_specs=[whole] + [pl.BlockSpec((2, rows, tile), lambda j: (0, 0, j))] * 3,
        compiler_params=pltpu.CompilerParams(vmem_limit_bytes=VMEM_LIMIT),
        cost_estimate=pl.CostEstimate(
            flops=12 * rows * features * width,
            bytes_accessed=4 * (rows * features + 3 * features * width + 3 * rows * width),
            transcendentals=2 * rows * width,
        ),
        name="hidden_units",
    )(h_own, h_other, cot, weights, weights, weights)


def run_jobs(name, scalars, jobs):
    starts, steps = [], 0
    for job in jobs:
        starts.append(steps)
        steps += job[0]
    in_specs, out_specs, shapes, args, counts = [], [], [], [], []

    def spec(block, index, start, size):
        return pl.BlockSpec(block, lambda t, s: index(jnp.clip(t - start, 0, size - 1), s))

    for start, (size, inputs, outputs, _) in zip(starts, jobs):
        for array, block, index in inputs:
            in_specs.append(spec(block, index, start, size))
            args.append(array)
        for shape, dtype, block, index in outputs:
            out_specs.append(spec(block, index, start, size))
            shapes.append(jax.ShapeDtypeStruct(shape, dtype))
        counts.append((len(inputs), len(outputs)))

    def kernel(scalars_ref, *refs):
        ins, outs = list(refs[: len(in_specs)]), list(refs[len(in_specs) :])
        step = pl.program_id(0)
        for start, (size, _, _, work), (n_in, n_out) in zip(starts, jobs, counts):
            mine, ins = ins[:n_in], ins[n_in:]
            made, outs = outs[:n_out], outs[n_out:]
            if len(jobs) == 1:
                work(step, scalars_ref, mine, made)
            else:
                pl.when((step >= start) & (step < start + size))(
                    functools.partial(work, step - start, scalars_ref, mine, made)
                )

    return pl.pallas_call(
        kernel,
        out_shape=shapes,
        grid_spec=pltpu.PrefetchScalarGridSpec(
            num_scalar_prefetch=1, grid=(steps,), in_specs=in_specs, out_specs=out_specs
        ),
        compiler_params=pltpu.CompilerParams(vmem_limit_bytes=VMEM_LIMIT),
        name=name,
    )(scalars, *args)


def sum_through(parts, weights, width):
    result = 0.0
    for part, weight in zip(parts, weights):
        for i in (0, 1):
            result = result + nt(part[i], weight[:, i].reshape(width, weight.shape[3]))
    return result


def back_job(parts, weights, matrices, rows_of, dtype, divide=1, block_of=None):
    blocks, _, chunk, _ = weights.shape
    _, rows, width = parts[0].shape
    features = blocks * chunk // divide
    tile = max(256, chunk)
    steps = features // tile
    if rows_of is not None:
        rows //= 2

    def at(j, s):
        return j if block_of is None else block_of(s) * steps + j

    inputs = [
        (part, (2, rows, width), lambda j, s: (0, 0 if rows_of is None else rows_of(s), 0))
        for part in parts
    ] + [
        (weights, (tile // chunk, 2, chunk, width), lambda j, s, m=m: (at(j, s), 0, 0, m))
        for m in matrices
    ]
    count = len(parts)

    def work(j, s, ins, outs):
        outs[0][...] = sum_through(ins[:count], ins[count:], tile).astype(dtype)

    return steps, inputs, [((rows, features), dtype, (rows, tile), lambda j, s: (0, j))], work


def back_tile(d_proj, weights, tokens, inverse, dots, gain, features):
    made = sum_through([d_proj], [weights], gain.shape[1]) * gain[...]
    scale = inverse[...] * (dots[0] + dots[1]) / features
    return made - tokens[...].astype(F32) * scale


def back_in_job(d_proj, weights, full, inverse, dots, gain, block_of, dtype):
    blocks, _, chunk, _ = weights.shape
    _, rows, width = d_proj.shape
    features = blocks * chunk
    tile = max(256, chunk)
    steps = features // tile // 2

    def at(j, s):
        return block_of(s) * steps + j

    inputs = [
        (d_proj, (2, rows, width), lambda j, s: (0, 0, 0)),
        (weights, (tile // chunk, 2, chunk, width), lambda j, s: (at(j, s), 0, 0, 0)),
        (full, (rows, tile), lambda j, s: (0, at(j, s))),
        (inverse, (rows, 1), lambda j, s: (0, 0)),
        (dots, (2, rows, 1), lambda j, s: (0, 0, 0)),
        (gain, (1, tile), lambda j, s: (0, at(j, s))),
    ]

    def work(j, s, ins, outs):
        outs[0][...] = back_tile(*ins, features).astype(dtype)

    outputs = [((rows, features // 2), dtype, (rows, tile), lambda j, s: (0, j))]
    return steps, inputs, outputs, work


def made_job(hidden, weights, matrix, residual):
    blocks, _, chunk, _ = weights.shape
    _, rows, width = hidden.shape
    features = blocks * chunk
    tile = max(256, chunk)
    steps = features // tile
    part = steps // 2
    height = residual.shape[0]

    def at(j, s):
        return jnp.where(j < part, (1 - s[1]) * part + j, s[1] * part + j - part)

    inputs = [
        (hidden, (2, rows, width), lambda j, s: (0, 0, 0)),
        (weights, (tile // chunk, 2, chunk, width), lambda j, s: (at(j, s), 0, 0, matrix)),
        (residual, (height, tile), lambda j, s: (0, at(j, s))),
    ]
    outputs = [
        ((rows, features // 2), BF16, (rows, tile), lambda j, s: (0, jnp.minimum(j, part - 1))),
        ((rows, features // 2), F32, (rows, tile), lambda j, s: (0, jnp.maximum(j - part, 0))),
    ]

    def work(j, s, ins, outs):
        result = sum_through(ins[:1], ins[1:2], tile)
        for out, mine in zip(outs, (j < part, j >= part)):

            @pl.when(mine)
            def _(out=out):
                out[:height, :] = (result[:height] + ins[2][...]).astype(out.dtype)
                out[height:, :] = result[height:].astype(out.dtype)

    return steps, inputs, outputs, work


def pair_job(left, right):
    rows, features = left.shape
    width = right.shape[2]
    tile = 256
    inputs = [
        (left, (rows, tile), lambda j, s: (0, j)),
        (right, (2, rows, width), lambda j, s: (0, 0, 0)),
    ]
    outputs = [((features, width), BF16, (tile, width), lambda j, s: (j, 0))] * 2

    def work(j, s, ins, outs):
        for i, index in enumerate((s[0], 1 - s[0])):
            outs[i][...] = tn(ins[0][...], ins[1][index]).astype(BF16)

    return features // tile, inputs, outputs, work


def norm_job(full, gain):
    rows, features = full.shape
    tile = rows // 4

    def work(j, s, ins, outs):
        value = ins[0][...].astype(F32)
        inverse = lax.rsqrt(jnp.mean(value * value, -1, keepdims=True) + EPS)
        outs[0][...] = (value * inverse * ins[1][...]).astype(BF16)
        outs[1][...] = inverse

    inputs = [
        (full, (tile, features), lambda j, s: (j, 0)),
        (gain, (1, features), lambda j, s: (0, 0)),
    ]
    outputs = [
        ((rows, features), BF16, (tile, features), lambda j, s: (j, 0)),
        ((rows, 1), F32, (tile, 1), lambda j, s: (j, 0)),
    ]
    return 4, inputs, outputs, work


def tail_job(h, weights, width):
    rows, features = h.shape
    blocks, _, chunk, _ = weights.shape

    def work(j, s, ins, outs):
        b, xin = (nn(ins[0][...], w[:, 0].reshape(features, width)) for w in ins[1:])
        outs[0][0] = (b * xin).astype(BF16)

    inputs = [(h, (8, features), lambda j, s: (rows // 8 - 1, 0))] + [
        (weights, (blocks, 1, chunk, width), lambda j, s, k=k: (0, j, 0, k)) for k in (0, 2)
    ]
    return 2, inputs, [((2, 8, width), BF16, (1, 8, width), lambda j, s: (j, 0, 0))], work


def project_job(h, weights, width):
    rows, features = h.shape
    blocks, _, chunk, _ = weights.shape
    def work(j, s, ins, outs):
        outs[0][0] = nn(ins[0][...], ins[1][:, 0].reshape(features, width))

    inputs = [
        (h, (rows, features), lambda j, s: (0, 0)),
        (weights, (blocks, 1, chunk, width), lambda j, s: (0, j // 3, 0, j % 3)),
    ]
    block = (1, rows, width)
    outputs = [((2, rows, 3 * width), F32, block, lambda j, s: (j // 3, 0, j % 3))]
    return 6, inputs, outputs, work


def mix_job(proj, edge, taps, weights):
    _, rows, width = proj.shape
    width //= 3
    half = rows // 2
    blocks, _, chunk, _ = weights.shape
    features = blocks * chunk
    tile = 256

    def core(j):
        return jnp.minimum(j, 1)

    def later(j):
        return jnp.maximum(j - 2, 0)

    inputs = [
        (proj, (1, rows, 3 * width), lambda j, s: (core(j), 0, 0)),
        (edge, (1, 2, width), lambda j, s: (core(j), 0, 0)),
        (taps, (1, 3, width), lambda j, s: (core(j), 0, 0)),
        (weights, (tile // chunk, 2, chunk, width), lambda j, s: (later(j), 0, 0, 3)),
    ]
    outputs = [
        ((2, rows, width), BF16, (2, rows, width), lambda j, s: (0, 0, 0)),
        ((half, features), BF16, (half, tile), lambda j, s: (0, later(j))),
    ]

    def work(j, s, ins, outs):
        values, before, filters, weight = ins

        @pl.when(j < 2)
        def _():
            b, gate, xin = (values[0, :, i * width : (i + 1) * width] for i in range(3))
            gated = (b * xin).astype(BF16).astype(F32)
            arriving = before[0].astype(F32)
            back = [shifted(gated, arriving, 2), shifted(gated, arriving, 1), gated]
            conv = sum(filters[0, k : k + 1, :] * back[k] for k in range(3))
            outs[0][j] = (gate * conv).astype(BF16)

        @pl.when(j >= 2)
        def _():
            start = pl.multiple_of((1 - s[1]) * half, half)
            made = 0.0
            for i in (0, 1):
                part = outs[0][i, pl.ds(start, half), :]
                made = made + nt(part, weight[:, i].reshape(tile, width))
            outs[1][...] = made.astype(BF16)

    return 2 + features // tile, inputs, outputs, work


def shifted(value, edge, distance):
    rows = value.shape[0]
    at = lax.broadcasted_iota(jnp.int32, value.shape, 0)
    moved = pltpu.roll(value, distance % rows, 0)
    if distance > 0:
        for i in range(distance):
            moved = jnp.where(at == i, edge[2 - distance + i : 3 - distance + i, :], moved)
    else:
        for i in range(-distance):
            moved = jnp.where(at == rows + distance + i, edge[i : i + 1, :], moved)
    return moved


def mixer_back_kernel(
    scalars,
    own,
    arrived,
    w_out,
    proj,
    edge,
    later,
    taps,
    h,
    mixed,
    w_in,
    tokens,
    inverse,
    gain,
    full,
    d_proj,
    dots,
    sums,
    grad_own,
    grad_other,
    gain_dots,
    sent,
):
    half = own.shape[0]
    width = w_out.shape[3]
    step = pl.program_id(0)
    core, rank = scalars[0], scalars[1]

    @pl.when(step == 0)
    def _():
        full[pl.ds(pl.multiple_of(rank * half, half), half), :] = own[...]
        full[pl.ds(pl.multiple_of((1 - rank) * half, half), half), :] = arrived[...]

    @pl.when(step < 2)
    def _():
        weight = w_out[:, 0].reshape(full.shape[1], width)
        d_y = nn(full[...], weight)
        b, gate, xin = (proj[0, :, i * width : (i + 1) * width] for i in range(3))
        gated = (b * xin).astype(BF16).astype(F32)
        before = edge[0].astype(F32)
        back = [shifted(gated, before, 2), shifted(gated, before, 1), gated]
        conv = sum(taps[0, k : k + 1, :] * back[k] for k in range(3))
        d_conv = (d_y * gate).astype(BF16).astype(F32)
        following = later[0].astype(F32)
        d_gated = (
            taps[0, 2:3, :] * d_conv
            + taps[0, 1:2, :] * shifted(d_conv, following, -1)
            + taps[0, 0:1, :] * shifted(d_conv, following, -2)
        )
        parts = [(d_gated * xin).astype(BF16), (d_y * conv).astype(BF16), (d_gated * b).astype(BF16)]
        for i, part in enumerate(parts):
            d_proj[step, :, i * width : (i + 1) * width] = part
        product = sum(part.astype(F32) * gate for part, gate in zip(parts, (b, gate, xin)))
        dots[step] = jnp.sum(product, -1, keepdims=True)
        rows = [jnp.sum(d_conv * value, 0, keepdims=True) for value in back]
        sums[0] = jnp.concatenate(rows + [jnp.zeros((5, width), F32)], 0)

    tiles = full.shape[1] // grad_own.shape[0]

    @pl.when((step >= 2) & (step < 2 + tiles))
    def _():
        tile = grad_own.shape[0]
        start = pl.multiple_of((step - 2) * tile, tile)
        dot = 0.0
        for out, index in ((grad_own, core), (grad_other, 1 - core)):
            made = tn(h[...], d_proj[index])
            out[:, : 3 * width] = made.astype(BF16)
            weight = w_in[:, index].reshape(made.shape).astype(F32)
            dot = dot + jnp.sum(made * weight, -1, keepdims=True)
            out[:, 3 * width :] = tn(full[:, pl.ds(start, tile)], mixed[index]).astype(BF16)
        gain_dots[...] = jnp.broadcast_to(dot, gain_dots.shape)

    @pl.when(step >= 2 + tiles)
    def _():
        sent[...] = back_tile(d_proj, w_in, tokens, inverse, dots, gain, full.shape[1]).astype(BF16)


def mixer_back(
    scalars, own, arrived, weights, proj, edge, later, taps, h, mixed, tokens, inverse, gain
):
    half, features = own.shape
    rows = 2 * half
    blocks, _, chunk, _ = weights.shape
    width = proj.shape[2] // 3
    tile = 256

    def per_core(shape):
        return pl.BlockSpec((1, *shape), lambda t, s: (jnp.minimum(t, 1), 0, 0))

    def whole(shape):
        return pl.BlockSpec(shape, lambda t, s: (0,) * len(shape))

    tiles = features // tile

    def tiled(block):
        return pl.BlockSpec(
            block, lambda t, s: (jnp.clip(t - 2, 0, tiles - 1),) + (0,) * (len(block) - 1)
        )

    def back(t, s):
        return (1 - s[1]) * (tiles // 2) + jnp.maximum(t - 2 - tiles, 0)

    def of_tile(t, s):
        return jnp.where(t < 2 + tiles, jnp.maximum(t - 2, 0), back(t, s))

    return pl.pallas_call(
        mixer_back_kernel,
        out_shape=[
            jax.ShapeDtypeStruct((rows, features), BF16),
            jax.ShapeDtypeStruct((2, rows, 3 * width), BF16),
            jax.ShapeDtypeStruct((2, rows, 1), F32),
            jax.ShapeDtypeStruct((2, 8, width), F32),
            jax.ShapeDtypeStruct((features, 4 * width), BF16),
            jax.ShapeDtypeStruct((features, 4 * width), BF16),
            jax.ShapeDtypeStruct((features, 128), F32),
            jax.ShapeDtypeStruct((rows, features // 2), BF16),
        ],
        grid_spec=pltpu.PrefetchScalarGridSpec(
            num_scalar_prefetch=1,
            grid=(2 + tiles + tiles // 2,),
            in_specs=[
                whole((half, features)),
                whole((half, features)),
                pl.BlockSpec((blocks, 1, chunk, width), lambda t, s: (0, jnp.minimum(t, 1), 0, 3)),
                per_core((rows, 3 * width)),
                per_core((2, width)),
                per_core((2, width)),
                per_core((3, width)),
                pl.BlockSpec((rows, tile), lambda t, s: (0, jnp.clip(t - 2, 0, tiles - 1))),
                whole((2, rows, width)),
                pl.BlockSpec(
                    (tile // chunk, 2, chunk, 3 * width), lambda t, s: (of_tile(t, s), 0, 0, 0)
                ),
                pl.BlockSpec((rows, tile), lambda t, s: (0, back(t, s))),
                whole((rows, 1)),
                pl.BlockSpec((1, tile), lambda t, s: (0, back(t, s))),
            ],
            out_specs=[
                whole((rows, features)),
                whole((2, rows, 3 * width)),
                whole((2, rows, 1)),
                per_core((8, width)),
                tiled((tile, 4 * width)),
                tiled((tile, 4 * width)),
                tiled((tile, 128)),
                pl.BlockSpec((rows, tile), lambda t, s: (0, jnp.maximum(t - 2 - tiles, 0))),
            ],
        ),
        compiler_params=pltpu.CompilerParams(vmem_limit_bytes=VMEM_LIMIT),
        name="mixer_back",
    )(
        scalars, own, arrived, weights, proj, edge, later, taps, h, mixed, weights, tokens, inverse, gain
    )


def body(
    tokens,
    in_weight,
    conv_kernel,
    out_weight,
    gate_weight,
    up_weight,
    down_weight,
    mixer_norm_gain,
    gain_ffn,
    cotangent,
):
    x, y, c = (lax.axis_index(name) for name in ("dp", "y", "c"))
    nx, nz = lax.axis_size("dp"), lax.axis_size("tok")
    width = tokens.shape[1]
    features = 4 * width
    rows = tokens.shape[0] // 2
    half = rows // 2
    chunk = in_weight.shape[0]
    pair = 2 * width
    scalars = jnp.stack([c, y, x])
    gain_row = mixer_norm_gain[None]

    def to_mp(value):
        mine, theirs = pick_rows(value, c, rows), pick_rows(value, 1 - c, rows)
        cross = [(2 * i + j, 2 * (1 - i) + 1 - j) for i in (0, 1) for j in (0, 1)]
        return mine, swap(theirs, "c"), swap(mine, "y"), lax.ppermute(theirs, ("y", "c"), cross)

    def join_mp(mine, beside, across, cross):
        near = by_rank(c, mine, beside, 1)
        return near, by_rank(y, near, by_rank(c, across, cross, 1), 1)

    every = ("dp", "tok", "c")

    def gather(shard):
        shard = with_layout_constraint(shard, Layout((0, 1)))
        whole = lax.all_gather(shard, every, axis=0, tiled=True)
        return whole.reshape(features // chunk, 2, chunk, shard.shape[1])

    first = jnp.concatenate([in_weight.reshape(chunk, 3 * width), out_weight.T], 1)
    first_tok = lax.all_to_all(
        jnp.concatenate([first] * nz, 0), "tok", split_axis=0, concat_axis=0, tiled=True
    )
    weights = jnp.concatenate([gate_weight, up_weight, down_weight.T], 1)
    pieces = to_mp(tokens)
    first_tok, weights, cotangent, *pieces = tie(first_tok, weights, cotangent, *pieces)
    weights = gather(weights)
    pieces_cot = to_mp(cotangent)
    taps = by_rank(c, conv_kernel[None], swap(conv_kernel, "c")[None]).astype(F32)

    def both_cores(part):
        mine, theirs = (v.reshape(-1, 1, chunk, v.shape[1]) for v in (part, swap(part, "c")))
        return by_rank(c, mine, theirs, 1)

    if nx == 2:
        first_dp = swap(first_tok, "dp")
        first_tok = both_cores(first_tok)
    else:
        first = lax.all_gather(both_cores(first_tok), "dp", axis=0, tiled=True)

    _, full = join_mp(*pieces)
    h_mix, inverse_mix = run_jobs("norm", scalars, [norm_job(full, gain_row)])
    if nx == 2:
        first_dp, first_tok, h_mix, *pieces_cot = tie(first_dp, first_tok, h_mix, *pieces_cot)
        first = by_rank(x, first_tok, both_cores(first_dp))
    _, cot = join_mp(*pieces_cot)
    cot = jnp.concatenate([pick_rows(cot, y, half), pick_rows(cot, 1 - y, half)], 0)

    ranks = nz * 2
    [gated] = run_jobs("tail", scalars, [tail_job(h_mix, first, width)])
    edge = lax.ppermute(gated[:, -2:], ("tok", "c"), [(i, i + 1) for i in range(ranks - 1)])
    [proj] = run_jobs("project", scalars, [project_job(h_mix, first, width)])
    gate_c = proj[:, :8, width : 2 * width]
    edge, proj = tie(edge, proj)
    mixed_in, sent = run_jobs("mix", scalars, [mix_job(proj, edge, taps, first)])

    def own_rows(s):
        return s[1]

    def other_rows(s):
        return 1 - s[1]

    arrived = swap(sent, "y")
    [kept] = run_jobs(
        "project_out", scalars, [back_job((mixed_in,), first, (3,), own_rows, F32)]
    )
    residual = pick_rows(full, y, half).astype(F32) + kept + arrived.astype(F32)

    inverse_ffn = lax.rsqrt(jnp.mean(residual * residual, -1, keepdims=True) + EPS)
    normalized = residual * inverse_ffn
    h_own = (normalized * gain_ffn).astype(BF16)
    h, hidden, d_gate, d_up = hidden_units(h_own, swap(h_own, "y"), cot, weights)

    def of_core(other):
        return swap(other, "c")

    down_own, down_other = run_jobs("down_gradient", scalars, [pair_job(cot, hidden)])
    d_gate, d_up, down_own, down_other = tie(d_gate, d_up, down_own, down_other)
    both = (d_gate, d_up)
    down_other = of_core(down_other)
    [sent] = run_jobs(
        "back_hidden", scalars, [back_job(both, weights, (0, 1), lambda s: 1, BF16)]
    )
    sent, down_own, down_other = tie(sent, down_own, down_other)

    late_gate, sent, *pieces = tie(d_gate, sent, *for_dp(down_own, down_other))
    arrived, pieces = swap(sent, "y"), to_dp(pieces)
    own, other, kept = run_jobs(
        "gate_gradient",
        scalars,
        [pair_job(h, late_gate), back_job(both, weights, (0, 1), lambda s: 0, F32)],
    )
    arrived, own, other, *pieces = tie(arrived, own, other, *pieces)
    other = of_core(other)
    d_h = kept + arrived.astype(F32)
    grad_gain_ffn = jnp.sum(d_h * normalized, 0)
    scaled = d_h * gain_ffn
    d_res = cot[:half].astype(F32) + inverse_ffn * (
        scaled - normalized * jnp.mean(scaled * normalized, -1, keepdims=True)
    )
    d_res_own = d_res.astype(BF16)
    down_mine = add_dp(down_own, down_other, pieces)
    late_up, late_hidden, d_res_own, down_mine, *pieces = tie(
        d_up, hidden, d_res_own, down_mine, *for_dp(own, other)
    )
    arrived, down_got, pieces = swap(d_res_own, "y"), to_tok(down_mine), to_dp(pieces)
    up_own, up_other, made_sent, made_kept = run_jobs(
        "up_gradient",
        scalars,
        [pair_job(h, late_up), made_job(late_hidden, weights, 2, residual)],
    )
    arrived, up_own, up_other, made_sent, made_kept, down_got, *pieces = tie(
        arrived, up_own, up_other, made_sent, made_kept, down_got, *pieces
    )
    up_other = of_core(up_other)
    gate_mine = add_dp(own, other, pieces)

    head = jnp.where(y == 0, d_res_own[:8], arrived[:8])
    w_out = first[:, :, :, 3 * width :]
    d_head = jnp.stack([nn(head, w_out[:, i].reshape(features, width)) for i in (0, 1)])
    d_head = (d_head * gate_c).astype(BF16)[:, :2]
    later = lax.ppermute(d_head, ("tok", "c"), [(i + 1, i) for i in range(ranks - 1)])
    arrived, gate_mine, later, *pieces = tie(
        arrived, gate_mine, later, *for_dp(up_own, up_other)
    )
    gate_got, pieces = to_tok(gate_mine), to_dp(pieces)
    d_res_full, d_proj, dots, grad_taps, own, other, gain_dots, sent = mixer_back(
        scalars,
        d_res_own,
        arrived,
        first,
        proj,
        edge,
        later,
        taps,
        h_mix,
        mixed_in,
        full,
        inverse_mix,
        gain_row,
    )
    near_sums = jnp.concatenate([grad_taps[0, :3], grad_taps[1, :3]], 1)
    sums = lax.dynamic_update_slice(jnp.zeros((3, features), F32), near_sums, (0, y * pair))
    gain_sum = gain_dots[:, 0] / mixer_norm_gain
    sums = jnp.concatenate([sums, gain_sum[None], grad_gain_ffn[None]], 0)
    d_proj, own, other, sent, gate_got, *pieces = tie(
        d_proj, own, other, sent, gate_got, *pieces
    )
    other, sums = of_core(other), sum_over(sums, "c")
    up_mine = add_dp(up_own, up_other, pieces)
    sent, d_proj, up_mine, sums, *pieces = tie(
        sent, d_proj, up_mine, sums, *for_dp(own, other)
    )
    arrived, up_got, pieces = swap(sent, "y"), to_tok(up_mine), to_dp(pieces)
    if nx == 2:
        cross = [(2 * i + j, 2 * (1 - i) + 1 - j) for i in (0, 1) for j in (0, 1)]
        near, far = swap(sums, "y"), lax.ppermute(sums, ("dp", "y"), cross)
        sums = [sums, near, swap(sums, "dp"), far]
    else:
        sums = [sum_over(sum_over(sums, "dp"), "y")]
    [kept] = run_jobs(
        "back_in",
        scalars,
        [back_in_job(d_proj, first, full, inverse_mix, dots, gain_row, own_rows, F32)],
    )
    arrived, kept, up_got, sums, *pieces = tie(arrived, kept, up_got, sums, *pieces)
    sums = (sums[0] + sums[1]) + (sums[2] + sums[3]) if nx == 2 else sums[0]
    mixer_mine = add_dp(own, other, pieces)

    high = sums.astype(BF16)
    low = (sums - high.astype(F32)).astype(BF16)
    extra = jnp.concatenate([high, low, jnp.zeros((16 - 2 * sums.shape[0], features), BF16)], 0)
    mixer_mine = jnp.concatenate(
        [
            mixer_mine.reshape(nz, chunk, features),
            jnp.broadcast_to(extra, (nz, 16, features)),
        ],
        1,
    )
    mixer_got = to_tok(mixer_mine.reshape(nz * (chunk + 16), features))
    made_sent, arrived = tie(made_sent, arrived)
    made_arrived = swap(made_sent, "y")

    d_res_near = jnp.where(y == 0, d_res_full[:, :pair], d_res_full[:, pair:]).astype(F32)

    def by_core(value):
        mine = jnp.where(c == 0, value[:, :width], value[:, width:])
        theirs = jnp.where(c == 0, value[:, width:], value[:, :width])
        return by_rank(c, mine, swap(theirs, "c"))

    input_gradient = by_core(
        d_res_near + inverse_mix * (kept + arrived.astype(F32))
    )
    out_near = by_rank(
        y,
        (made_kept[:half] + made_arrived[half:].astype(F32)).astype(BF16),
        (made_kept[half:] + made_arrived[:half].astype(F32)).astype(BF16),
    )
    mixed = by_core(out_near)
    grad_down, grad_gate, grad_up = (add_tok(v) for v in (down_got, gate_got, up_got))
    mixer_sum = add_tok(mixer_got)
    grad_mixer = mixer_sum[:chunk]
    sums = mixer_sum[chunk : chunk + 5] + mixer_sum[chunk + 5 : chunk + 10]
    grad_in = grad_mixer[:, : 3 * width].reshape(chunk, 3, width)
    grad_out = grad_mixer[:, 3 * width :].T

    sums = lax.dynamic_slice_in_dim(sums, (2 * y + c) * width, width, 1)

    return (
        mixed,
        input_gradient,
        grad_in,
        sums[:3],
        grad_out,
        grad_gate,
        grad_up,
        grad_down.T,
        sums[3],
        sums[4],
    )


def solution(mesh):
    split = Mesh(
        mesh.devices.reshape(mesh.shape["dp"], mesh.shape["tok"], mesh.shape["mp"] // 2, 2),
        ("dp", "tok", "y", "c"),
    )
    tok, mp = ("dp", "tok"), ("y", "c")
    return jax.shard_map(
        body,
        mesh=split,
        in_specs=(
            P(tok, mp),
            P(tok, None, mp),
            P(None, mp),
            P(mp, tok),
            P(tok, mp),
            P(tok, mp),
            P(mp, tok),
            P(),
            P(),
            P(tok, mp),
        ),
        out_specs=(
            P(tok, mp),
            P(tok, mp),
            P(tok, None, mp),
            P(None, mp),
            P(mp, tok),
            P(tok, mp),
            P(tok, mp),
            P(mp, tok),
            P(mp),
            P(mp),
        ),
        check_vma=False,
    )
```

```python
import functools

import jax
import jax.numpy as jnp
from jax import lax
from jax.experimental import pallas as pl
from jax.experimental.layout import Layout, with_layout_constraint
from jax.experimental.pallas import tpu as pltpu
from jax.sharding import Mesh
from jax.sharding import PartitionSpec as P

EPS = 1e-05
F32 = jnp.float32
BF16 = jnp.bfloat16
VMEM_LIMIT = 56 * 2**20


def swap(value, axis):
    return lax.ppermute(value, axis, [(0, 1), (1, 0)])


def deliver(value, axis, distance):
    size = lax.axis_size(axis)
    return lax.ppermute(value, axis, [(s, (s + distance) % size) for s in range(size)])


def dot(left, right, contract):
    return lax.dot_general(left, right, (contract, ((), ())), preferred_element_type=F32)


def nn(left, right):
    return dot(left, right, ((1,), (0,)))


def nt(left, right):
    return dot(left, right, ((1,), (1,)))


def tn(left, right):
    return dot(left, right, ((0,), (0,)))


def total(values):
    result = values[0].astype(F32)
    for value in values[1:]:
        result = result + value.astype(F32)
    return result


def tie(*values):
    return lax.optimization_barrier(values)


def pick_rows(value, index, size):
    return lax.dynamic_slice_in_dim(value, index * size, size, 0)


def by_rank(index, first, second, axis=0):
    return jnp.where(
        index == 0,
        jnp.concatenate([first, second], axis),
        jnp.concatenate([second, first], axis),
    )


def for_dp(own, other):
    steps = lax.axis_size("dp")
    size = own.shape[0] // steps
    indices = [(lax.axis_index("dp") + i) % steps for i in range(1, steps)]
    return [
        total([pick_rows(part, index, size) for part in (own, other)]).astype(BF16)
        for index in indices
    ]


def to_dp(pieces):
    return [deliver(piece, "dp", i + 1) for i, piece in enumerate(pieces)]


def to_tok(mine):
    return lax.all_to_all(mine, "tok", split_axis=0, concat_axis=0, tiled=True)


def add_tok(got):
    steps = lax.axis_size("tok")
    size = got.shape[0] // steps
    return total([got[i * size : (i + 1) * size] for i in range(steps)])


def for_self(own, other):
    size = own.shape[0] // lax.axis_size("dp")
    mine = [pick_rows(part, lax.axis_index("dp"), size) for part in (own, other)]
    return total(mine).astype(BF16)


def add_dp(keep, arrived):
    return total([keep, *arrived]).astype(BF16)


def sum_over(value, axis):
    size = lax.axis_size(axis)
    if size & (size - 1):
        return lax.psum(value, axis)
    step = 1
    while step < size:
        value = value + lax.ppermute(value, axis, [(s, s ^ step) for s in range(size)])
        step *= 2
    return value


def hidden_kernel(scalars, h_own, h_other, cot, w_gate, w_up, w_down, h, *outs):
    features = h.shape[1]
    half = h_own.shape[0]

    @pl.when(pl.program_id(0) == 0)
    def _():
        h[:half, :] = h_own[...]
        h[half:, :] = h_other[...]

    core = scalars[0]

    def both(w):
        return jnp.concatenate(
            [w[:, i].reshape(features, w.shape[3]) for i in (core, 1 - core)], 1
        )

    w_gate, w_up, w_down = both(w_gate), both(w_up), both(w_down)
    width = w_gate.shape[1] // 2
    step = 256
    for start in range(0, h.shape[0], step):
        part = pl.ds(start, step)
        gate, up = nn(h[part, :], w_gate), nn(h[part, :], w_up)
        d_hidden = nn(cot[part, :], w_down)
        sigma = jax.nn.sigmoid(gate)
        silu = gate * sigma
        results = (
            silu * up,
            d_hidden * up * sigma * (1.0 + gate * (1.0 - sigma)),
            d_hidden * silu,
        )
        for i, value in enumerate(results):
            value = value.astype(BF16)
            outs[2 * i][part, :] = value[:, :width]
            outs[2 * i + 1][part, :] = value[:, width:]


def hidden_units(scalars, h_own, h_other, cot, weights):
    rows, features = cot.shape
    blocks, _, chunk, width = weights.shape
    width //= 3
    tile = 128
    tiles = width // tile

    def of(matrix):
        return pl.BlockSpec((blocks, 2, chunk, tile), lambda j, s: (0, 0, 0, matrix * tiles + j))

    whole = pl.BlockSpec((rows, features), lambda j, s: (0, 0))
    half = pl.BlockSpec((rows // 2, features), lambda j, s: (0, 0))
    return pl.pallas_call(
        hidden_kernel,
        out_shape=[jax.ShapeDtypeStruct((rows, features), BF16)]
        + [jax.ShapeDtypeStruct((rows, width), BF16)] * 6,
        grid_spec=pltpu.PrefetchScalarGridSpec(
            num_scalar_prefetch=1,
            grid=(tiles,),
            in_specs=[half, half, whole, of(0), of(1), of(2)],
            out_specs=[whole] + [pl.BlockSpec((rows, tile), lambda j, s: (0, j))] * 6,
        ),
        compiler_params=pltpu.CompilerParams(vmem_limit_bytes=VMEM_LIMIT),
        name="hidden_units",
    )(scalars, h_own, h_other, cot, weights, weights, weights)


def run_jobs(name, scalars, jobs, limit=56):
    starts, steps = [], 0
    for job in jobs:
        starts.append(steps)
        steps += job[0]
    in_specs, out_specs, shapes, args, counts = [], [], [], [], []

    def spec(block, index, start, size):
        return pl.BlockSpec(block, lambda t, s: index(jnp.clip(t - start, 0, size - 1), s))

    for start, (size, inputs, outputs, _) in zip(starts, jobs):
        for array, block, index in inputs:
            in_specs.append(spec(block, index, start, size))
            args.append(array)
        for shape, dtype, block, index in outputs:
            out_specs.append(spec(block, index, start, size))
            shapes.append(jax.ShapeDtypeStruct(shape, dtype))
        counts.append((len(inputs), len(outputs)))

    def kernel(scalars_ref, *refs):
        ins, outs = list(refs[: len(in_specs)]), list(refs[len(in_specs) :])
        step = pl.program_id(0)
        for start, (size, _, _, work), (n_in, n_out) in zip(starts, jobs, counts):
            mine, ins = ins[:n_in], ins[n_in:]
            made, outs = outs[:n_out], outs[n_out:]
            if len(jobs) == 1:
                work(step, scalars_ref, mine, made)
            else:
                pl.when((step >= start) & (step < start + size))(
                    functools.partial(work, step - start, scalars_ref, mine, made)
                )

    return pl.pallas_call(
        kernel,
        out_shape=shapes,
        grid_spec=pltpu.PrefetchScalarGridSpec(
            num_scalar_prefetch=1, grid=(steps,), in_specs=in_specs, out_specs=out_specs
        ),
        compiler_params=pltpu.CompilerParams(vmem_limit_bytes=limit * 2**20),
        name=name,
    )(scalars, *args)


def sum_through(parts, weights, width):
    result = 0.0
    for part, weight in zip(parts, weights):
        for i in (0, 1):
            result = result + nt(part[i], weight[:, i].reshape(width, weight.shape[3]))
    return result


def sum_pairs(core, parts, weights, width):
    result = 0.0
    for i, weight in enumerate(weights):
        for part, index in ((parts[2 * i], core), (parts[2 * i + 1], 1 - core)):
            result = result + nt(part[...], weight[:, index].reshape(width, weight.shape[3]))
    return result


def hidden_back_job(pairs, weights, matrices, half):
    blocks, _, chunk, _ = weights.shape
    rows, width = pairs[0].shape
    rows //= 2
    features = blocks * chunk
    tile = max(256, chunk)
    inputs = [(part, (rows, width), lambda j, s: (half, 0)) for part in pairs] + [
        (weights, (tile // chunk, 2, chunk, width), lambda j, s, m=m: (j, 0, 0, m))
        for m in matrices
    ]
    count = len(pairs)

    def work(j, s, ins, outs):
        outs[0][...] = sum_pairs(s[0], ins[:count], ins[count:], tile).astype(BF16)

    outputs = [((rows, features), BF16, (rows, tile), lambda j, s: (0, j))]
    return features // tile, inputs, outputs, work


def back_job(parts, weights, matrices, rows_of, dtype, divide=1, block_of=None):
    blocks, _, chunk, _ = weights.shape
    _, rows, width = parts[0].shape
    features = blocks * chunk // divide
    tile = max(256, chunk)
    steps = features // tile
    if rows_of is not None:
        rows //= 2

    def at(j, s):
        return j if block_of is None else block_of(s) * steps + j

    inputs = [
        (part, (2, rows, width), lambda j, s: (0, 0 if rows_of is None else rows_of(s), 0))
        for part in parts
    ] + [
        (weights, (tile // chunk, 2, chunk, width), lambda j, s, m=m: (at(j, s), 0, 0, m))
        for m in matrices
    ]
    count = len(parts)

    def work(j, s, ins, outs):
        outs[0][...] = sum_through(ins[:count], ins[count:], tile).astype(dtype)

    return steps, inputs, [((rows, features), dtype, (rows, tile), lambda j, s: (0, j))], work


def back_tile(d_proj, weights, tokens, inverse, dots, gain, features):
    made = sum_through([d_proj], [weights], gain.shape[1]) * gain[...]
    scale = inverse[...] * (dots[0] + dots[1]) / features
    return made - tokens[...].astype(F32) * scale


def back_in_job(d_proj, weights, full, inverse, dots, gain, block_of, dtype):
    blocks, _, chunk, _ = weights.shape
    _, rows, width = d_proj.shape
    features = blocks * chunk
    tile = max(256, chunk)
    steps = features // tile // 2

    def at(j, s):
        return block_of(s) * steps + j

    inputs = [
        (d_proj, (2, rows, width), lambda j, s: (0, 0, 0)),
        (weights, (tile // chunk, 2, chunk, width), lambda j, s: (at(j, s), 0, 0, 0)),
        (full, (rows, tile), lambda j, s: (0, at(j, s))),
        (inverse, (rows, 1), lambda j, s: (0, 0)),
        (dots, (2, rows, 1), lambda j, s: (0, 0, 0)),
        (gain, (1, tile), lambda j, s: (0, at(j, s))),
    ]

    def work(j, s, ins, outs):
        outs[0][...] = back_tile(*ins, features).astype(dtype)

    outputs = [((rows, features // 2), dtype, (rows, tile), lambda j, s: (0, j))]
    return steps, inputs, outputs, work


def made_job(hidden, weights, matrix, residual):
    blocks, _, chunk, _ = weights.shape
    rows, width = hidden[0].shape
    features = blocks * chunk
    tile = max(256, chunk)
    steps = features // tile
    part = steps // 2
    height = residual.shape[0]

    def at(j, s):
        return jnp.where(j < part, (1 - s[1]) * part + j, s[1] * part + j - part)

    inputs = [(value, (rows, width), lambda j, s: (0, 0)) for value in hidden] + [
        (weights, (tile // chunk, 2, chunk, width), lambda j, s: (at(j, s), 0, 0, matrix)),
        (residual, (height, tile), lambda j, s: (0, at(j, s))),
    ]
    outputs = [
        ((rows, features // 2), BF16, (rows, tile), lambda j, s: (0, jnp.minimum(j, part - 1))),
        ((rows, features // 2), F32, (rows, tile), lambda j, s: (0, jnp.maximum(j - part, 0))),
    ]

    def work(j, s, ins, outs):
        result = sum_pairs(s[0], ins[:2], ins[2:3], tile)
        for out, mine in zip(outs, (j < part, j >= part)):

            @pl.when(mine)
            def _(out=out):
                out[:height, :] = (result[:height] + ins[3][...]).astype(out.dtype)
                out[height:, :] = result[height:].astype(out.dtype)

    return steps, inputs, outputs, work


def gradient_job(lefts, rights, devices):
    rows, features = lefts[0].shape
    width = rights[0].shape[1]
    size = features // devices
    tile = min(256, size)
    steps, mine = features // tile, size // tile
    inputs = [
        (left, (rows, tile), lambda j, s: (0, lax.rem(s[2] * mine + j, steps))) for left in lefts
    ] + [(right, (rows, width), lambda j, s: (0, 0)) for right in rights]
    outputs = [
        ((size, width), BF16, (tile, width), lambda j, s: (jnp.minimum(j, mine - 1), 0)),
        ((features - size, width), BF16, (tile, width), lambda j, s: (jnp.maximum(j - mine, 0), 0)),
    ]

    def work(j, s, ins, outs):
        made = (tn(ins[0][...], ins[2][...]) + tn(ins[1][...], ins[3][...])).astype(BF16)

        @pl.when(j < mine)
        def _():
            outs[0][...] = made

        @pl.when(j >= mine)
        def _():
            outs[1][...] = made

    return steps, inputs, outputs, work


def norm_job(full, gain):
    rows, features = full.shape
    tile = rows // 4

    def work(j, s, ins, outs):
        value = ins[0][...].astype(F32)
        inverse = lax.rsqrt(jnp.mean(value * value, -1, keepdims=True) + EPS)
        outs[0][...] = (value * inverse * ins[1][...]).astype(BF16)
        outs[1][...] = inverse

    inputs = [
        (full, (tile, features), lambda j, s: (j, 0)),
        (gain, (1, features), lambda j, s: (0, 0)),
    ]
    outputs = [
        ((rows, features), BF16, (tile, features), lambda j, s: (j, 0)),
        ((rows, 1), F32, (tile, 1), lambda j, s: (j, 0)),
    ]
    return 4, inputs, outputs, work


def tail_job(h, weights, width):
    rows, features = h.shape
    blocks, _, chunk, _ = weights.shape

    def work(j, s, ins, outs):
        b, xin = (nn(ins[0][...], w[:, 0].reshape(features, width)) for w in ins[1:])
        outs[0][0] = (b * xin).astype(BF16)

    inputs = [(h, (8, features), lambda j, s: (rows // 8 - 1, 0))] + [
        (weights, (blocks, 1, chunk, width), lambda j, s, k=k: (0, j, 0, k)) for k in (0, 2)
    ]
    return 2, inputs, [((2, 8, width), BF16, (1, 8, width), lambda j, s: (j, 0, 0))], work


def project_job(h, weights, width):
    rows, features = h.shape
    blocks, _, chunk, _ = weights.shape
    def work(j, s, ins, outs):
        outs[0][0] = nn(ins[0][...], ins[1][:, 0].reshape(features, width))

    inputs = [
        (h, (rows, features), lambda j, s: (0, 0)),
        (weights, (blocks, 1, chunk, width), lambda j, s: (0, j // 3, 0, j % 3)),
    ]
    block = (1, rows, width)
    outputs = [((2, rows, 3 * width), F32, block, lambda j, s: (j // 3, 0, j % 3))]
    return 6, inputs, outputs, work


def mix_job(proj, edge, taps, weights):
    _, rows, width = proj.shape
    width //= 3
    half = rows // 2
    blocks, _, chunk, _ = weights.shape
    features = blocks * chunk
    tile = 256

    def core(j):
        return jnp.minimum(j, 1)

    def later(j):
        return jnp.maximum(j - 2, 0)

    inputs = [
        (proj, (1, rows, 3 * width), lambda j, s: (core(j), 0, 0)),
        (edge, (1, 2, width), lambda j, s: (core(j), 0, 0)),
        (taps, (1, 3, width), lambda j, s: (core(j), 0, 0)),
        (weights, (tile // chunk, 2, chunk, width), lambda j, s: (later(j), 0, 0, 3)),
    ]
    outputs = [
        ((2, rows, width), BF16, (2, rows, width), lambda j, s: (0, 0, 0)),
        ((half, features), BF16, (half, tile), lambda j, s: (0, later(j))),
    ]

    def work(j, s, ins, outs):
        values, before, filters, weight = ins

        @pl.when(j < 2)
        def _():
            b, gate, xin = (values[0, :, i * width : (i + 1) * width] for i in range(3))
            gated = (b * xin).astype(BF16).astype(F32)
            arriving = before[0].astype(F32)
            back = [shifted(gated, arriving, 2), shifted(gated, arriving, 1), gated]
            conv = sum(filters[0, k : k + 1, :] * back[k] for k in range(3))
            outs[0][j] = (gate * conv).astype(BF16)

        @pl.when(j >= 2)
        def _():
            start = pl.multiple_of((1 - s[1]) * half, half)
            made = 0.0
            for i in (0, 1):
                part = outs[0][i, pl.ds(start, half), :]
                made = made + nt(part, weight[:, i].reshape(tile, width))
            outs[1][...] = made.astype(BF16)

    return 2 + features // tile, inputs, outputs, work


def shifted(value, edge, distance):
    rows = value.shape[0]
    at = lax.broadcasted_iota(jnp.int32, value.shape, 0)
    moved = pltpu.roll(value, distance % rows, 0)
    if distance > 0:
        for i in range(distance):
            moved = jnp.where(at == i, edge[2 - distance + i : 3 - distance + i, :], moved)
    else:
        for i in range(-distance):
            moved = jnp.where(at == rows + distance + i, edge[i : i + 1, :], moved)
    return moved


def mixer_back_kernel(
    scalars,
    own,
    arrived,
    w_out,
    proj,
    edge,
    later,
    taps,
    h,
    mixed,
    w_in,
    tokens,
    inverse,
    gain,
    full,
    d_proj,
    dots,
    sums,
    grad_own,
    grad_other,
    gain_dots,
    sent,
):
    half = own.shape[0]
    width = w_out.shape[3]
    step = pl.program_id(0)
    core, rank = scalars[0], scalars[1]

    @pl.when(step == 0)
    def _():
        full[pl.ds(pl.multiple_of(rank * half, half), half), :] = own[...]
        full[pl.ds(pl.multiple_of((1 - rank) * half, half), half), :] = arrived[...]

    @pl.when(step < 2)
    def _():
        weight = w_out[:, 0].reshape(full.shape[1], width)
        d_y = nn(full[...], weight)
        b, gate, xin = (proj[0, :, i * width : (i + 1) * width] for i in range(3))
        gated = (b * xin).astype(BF16).astype(F32)
        before = edge[0].astype(F32)
        back = [shifted(gated, before, 2), shifted(gated, before, 1), gated]
        conv = sum(taps[0, k : k + 1, :] * back[k] for k in range(3))
        d_conv = (d_y * gate).astype(BF16).astype(F32)
        following = later[0].astype(F32)
        d_gated = (
            taps[0, 2:3, :] * d_conv
            + taps[0, 1:2, :] * shifted(d_conv, following, -1)
            + taps[0, 0:1, :] * shifted(d_conv, following, -2)
        )
        parts = [(d_gated * xin).astype(BF16), (d_y * conv).astype(BF16), (d_gated * b).astype(BF16)]
        for i, part in enumerate(parts):
            d_proj[step, :, i * width : (i + 1) * width] = part
        product = sum(part.astype(F32) * gate for part, gate in zip(parts, (b, gate, xin)))
        dots[step] = jnp.sum(product, -1, keepdims=True)
        rows = [jnp.sum(d_conv * value, 0, keepdims=True) for value in back]
        sums[0] = jnp.concatenate(rows + [jnp.zeros((5, width), F32)], 0)

    tiles = full.shape[1] // grad_own.shape[0]

    @pl.when((step >= 2) & (step < 2 + tiles))
    def _():
        tile = grad_own.shape[0]
        start = pl.multiple_of((step - 2) * tile, tile)
        dot = 0.0
        for out, index in ((grad_own, core), (grad_other, 1 - core)):
            made = tn(h[...], d_proj[index])
            out[:, : 3 * width] = made.astype(BF16)
            weight = w_in[:, index].reshape(made.shape).astype(F32)
            dot = dot + jnp.sum(made * weight, -1, keepdims=True)
            out[:, 3 * width :] = tn(full[:, pl.ds(start, tile)], mixed[index]).astype(BF16)
        gain_dots[...] = jnp.broadcast_to(dot, gain_dots.shape)

    @pl.when(step >= 2 + tiles)
    def _():
        sent[...] = back_tile(d_proj, w_in, tokens, inverse, dots, gain, full.shape[1]).astype(BF16)


def mixer_back(
    scalars, own, arrived, weights, proj, edge, later, taps, h, mixed, tokens, inverse, gain
):
    half, features = own.shape
    rows = 2 * half
    blocks, _, chunk, _ = weights.shape
    width = proj.shape[2] // 3
    tile = 256

    def per_core(shape):
        return pl.BlockSpec((1, *shape), lambda t, s: (jnp.minimum(t, 1), 0, 0))

    def whole(shape):
        return pl.BlockSpec(shape, lambda t, s: (0,) * len(shape))

    tiles = features // tile

    def tiled(block):
        return pl.BlockSpec(
            block, lambda t, s: (jnp.clip(t - 2, 0, tiles - 1),) + (0,) * (len(block) - 1)
        )

    def back(t, s):
        return (1 - s[1]) * (tiles // 2) + jnp.maximum(t - 2 - tiles, 0)

    def of_tile(t, s):
        return jnp.where(t < 2 + tiles, jnp.maximum(t - 2, 0), back(t, s))

    return pl.pallas_call(
        mixer_back_kernel,
        out_shape=[
            jax.ShapeDtypeStruct((rows, features), BF16),
            jax.ShapeDtypeStruct((2, rows, 3 * width), BF16),
            jax.ShapeDtypeStruct((2, rows, 1), F32),
            jax.ShapeDtypeStruct((2, 8, width), F32),
            jax.ShapeDtypeStruct((features, 4 * width), BF16),
            jax.ShapeDtypeStruct((features, 4 * width), BF16),
            jax.ShapeDtypeStruct((features, 128), F32),
            jax.ShapeDtypeStruct((rows, features // 2), BF16),
        ],
        grid_spec=pltpu.PrefetchScalarGridSpec(
            num_scalar_prefetch=1,
            grid=(2 + tiles + tiles // 2,),
            in_specs=[
                whole((half, features)),
                whole((half, features)),
                pl.BlockSpec((blocks, 1, chunk, width), lambda t, s: (0, jnp.minimum(t, 1), 0, 3)),
                per_core((rows, 3 * width)),
                per_core((2, width)),
                per_core((2, width)),
                per_core((3, width)),
                pl.BlockSpec((rows, tile), lambda t, s: (0, jnp.clip(t - 2, 0, tiles - 1))),
                whole((2, rows, width)),
                pl.BlockSpec(
                    (tile // chunk, 2, chunk, 3 * width), lambda t, s: (of_tile(t, s), 0, 0, 0)
                ),
                pl.BlockSpec((rows, tile), lambda t, s: (0, back(t, s))),
                whole((rows, 1)),
                pl.BlockSpec((1, tile), lambda t, s: (0, back(t, s))),
            ],
            out_specs=[
                whole((rows, features)),
                whole((2, rows, 3 * width)),
                whole((2, rows, 1)),
                per_core((8, width)),
                tiled((tile, 4 * width)),
                tiled((tile, 4 * width)),
                tiled((tile, 128)),
                pl.BlockSpec((rows, tile), lambda t, s: (0, jnp.maximum(t - 2 - tiles, 0))),
            ],
        ),
        compiler_params=pltpu.CompilerParams(vmem_limit_bytes=VMEM_LIMIT),
        name="mixer_back",
    )(
        scalars, own, arrived, weights, proj, edge, later, taps, h, mixed, weights, tokens, inverse, gain
    )


def body(
    tokens,
    in_weight,
    conv_kernel,
    out_weight,
    gate_weight,
    up_weight,
    down_weight,
    mixer_norm_gain,
    gain_ffn,
    cotangent,
):
    x, y, c = (lax.axis_index(name) for name in ("dp", "y", "c"))
    nx, nz = lax.axis_size("dp"), lax.axis_size("tok")
    width = tokens.shape[1]
    features = 4 * width
    rows = tokens.shape[0] // 2
    half = rows // 2
    chunk = in_weight.shape[0]
    pair = 2 * width
    scalars = jnp.stack([c, y, x])
    gain_row = mixer_norm_gain[None]

    def to_mp(value):
        mine, theirs = pick_rows(value, c, rows), pick_rows(value, 1 - c, rows)
        cross = [(2 * i + j, 2 * (1 - i) + 1 - j) for i in (0, 1) for j in (0, 1)]
        return mine, swap(theirs, "c"), swap(mine, "y"), lax.ppermute(theirs, ("y", "c"), cross)

    def join_mp(mine, beside, across, cross):
        near = by_rank(c, mine, beside, 1)
        return near, by_rank(y, near, by_rank(c, across, cross, 1), 1)

    every = ("dp", "tok", "c")

    def gather(shard):
        shard = with_layout_constraint(shard, Layout((0, 1)))
        whole = lax.all_gather(shard, every, axis=0, tiled=True)
        return whole.reshape(features // chunk, 2, chunk, shard.shape[1])

    first = jnp.concatenate([in_weight.reshape(chunk, 3 * width), out_weight.T], 1)
    first_tok = lax.all_to_all(
        jnp.concatenate([first] * nz, 0), "tok", split_axis=0, concat_axis=0, tiled=True
    )
    weights = jnp.concatenate([gate_weight, up_weight, down_weight.T], 1)
    pieces = to_mp(tokens)
    first_tok, weights, cotangent, *pieces = tie(first_tok, weights, cotangent, *pieces)
    weights = gather(weights)
    pieces_cot = to_mp(cotangent)
    taps = by_rank(c, conv_kernel[None], swap(conv_kernel, "c")[None]).astype(F32)

    def both_cores(part):
        mine, theirs = (v.reshape(-1, 1, chunk, v.shape[1]) for v in (part, swap(part, "c")))
        return by_rank(c, mine, theirs, 1)

    if nx == 2:
        first_dp = swap(first_tok, "dp")
        first_tok = both_cores(first_tok)
    else:
        first = lax.all_gather(both_cores(first_tok), "dp", axis=0, tiled=True)

    _, full = join_mp(*pieces)
    h_mix, inverse_mix = run_jobs("norm", scalars, [norm_job(full, gain_row)], 12)
    if nx == 2:
        first_dp, first_tok, h_mix, *pieces_cot = tie(first_dp, first_tok, h_mix, *pieces_cot)
        first = by_rank(x, first_tok, both_cores(first_dp))
    _, cot = join_mp(*pieces_cot)
    cot = jnp.concatenate([pick_rows(cot, y, half), pick_rows(cot, 1 - y, half)], 0)
    cot, cot_beside = tie(cot, swap(cot, "c"))

    ranks = nz * 2
    [gated] = run_jobs("tail", scalars, [tail_job(h_mix, first, width)], 16)
    edge = lax.ppermute(gated[:, -2:], ("tok", "c"), [(i, i + 1) for i in range(ranks - 1)])
    [proj] = run_jobs("project", scalars, [project_job(h_mix, first, width)], 20)
    gate_c = proj[:, :8, width : 2 * width]
    edge, proj = tie(edge, proj)
    mixed_in, sent = run_jobs("mix", scalars, [mix_job(proj, edge, taps, first)], 28)

    def own_rows(s):
        return s[1]

    def other_rows(s):
        return 1 - s[1]

    arrived = swap(sent, "y")
    [kept] = run_jobs(
        "project_out", scalars, [back_job((mixed_in,), first, (3,), own_rows, F32)], 20
    )
    w_out = [first[:, i, :, 3 * width :].reshape(features, width) for i in (0, 1)]
    arrived, kept, *w_out = tie(arrived, kept, *w_out)
    residual = pick_rows(full, y, half).astype(F32) + kept + arrived.astype(F32)

    inverse_ffn = lax.rsqrt(jnp.mean(residual * residual, -1, keepdims=True) + EPS)
    normalized = residual * inverse_ffn
    h_own = (normalized * gain_ffn).astype(BF16)
    h, *units = hidden_units(scalars, h_own, swap(h_own, "y"), cot, weights)
    hidden, d_gate, d_up = units[:2], units[2:4], units[4:]

    def of_core(other):
        return swap(other, "c")

    def pieces_of(send):
        size = features // nx
        return to_dp([send[i * size : (i + 1) * size] for i in range(nx - 1)])

    hidden_beside, h_beside = of_core(hidden[1]), of_core(h)
    [sent] = run_jobs(
        "back_hidden", scalars, [hidden_back_job([*d_gate, *d_up], weights, (0, 1), 1)]
    )
    sent, hidden_beside, h_beside, *units = tie(sent, hidden_beside, h_beside, *hidden, *d_gate, *d_up)
    hidden, d_gate, d_up = units[:2], units[2:4], units[4:]
    gate_beside, up_beside = of_core(d_gate[1]), of_core(d_up[1])
    keep, send = run_jobs(
        "down_gradient",
        scalars,
        [gradient_job([cot, cot_beside], [hidden[0], hidden_beside], nx)],
    )
    sent, keep, send, gate_beside, up_beside, *units = tie(
        sent, keep, send, gate_beside, up_beside, *hidden, *d_gate, *d_up
    )
    hidden, d_gate, d_up = units[:2], units[2:4], units[4:]
    arrived, pieces = swap(sent, "y"), pieces_of(send)
    next_keep, send, kept = run_jobs(
        "gate_gradient",
        scalars,
        [
            gradient_job([h, h_beside], [d_gate[0], gate_beside], nx),
            hidden_back_job([*d_gate, *d_up], weights, (0, 1), 0),
        ],
    )
    arrived, send, kept, *pieces = tie(arrived, send, kept, *pieces)
    d_h = kept.astype(F32) + arrived.astype(F32)
    grad_gain_ffn = jnp.sum(d_h * normalized, 0)
    scaled = d_h * gain_ffn
    d_res = cot[:half].astype(F32) + inverse_ffn * (
        scaled - normalized * jnp.mean(scaled * normalized, -1, keepdims=True)
    )
    d_res_own = d_res.astype(BF16)
    down_mine = add_dp(keep, pieces)
    d_res_own, down_mine, send, *units = tie(d_res_own, down_mine, send, *hidden, *d_up)
    hidden, d_up = units[:2], units[2:]
    arrived, down_got, pieces = swap(d_res_own, "y"), to_tok(down_mine), pieces_of(send)
    keep, send, made_sent, made_kept = run_jobs(
        "up_gradient",
        scalars,
        [
            gradient_job([h, h_beside], [d_up[0], up_beside], nx),
            made_job(hidden, weights, 2, residual),
        ],
    )
    arrived, send, made_sent, made_kept, down_got, *pieces = tie(
        arrived, send, made_sent, made_kept, down_got, *pieces
    )
    gate_mine = add_dp(next_keep, pieces)

    head = jnp.where(y == 0, d_res_own[:8], arrived[:8])
    d_head = jnp.stack([nn(head, w) for w in w_out])
    d_head = (d_head * gate_c).astype(BF16)[:, :2]
    later = lax.ppermute(d_head, ("tok", "c"), [(i + 1, i) for i in range(ranks - 1)])
    arrived, gate_mine, later, send = tie(arrived, gate_mine, later, send)
    gate_got, pieces = to_tok(gate_mine), pieces_of(send)
    d_res_full, d_proj, dots, grad_taps, own, other, gain_dots, sent = mixer_back(
        scalars,
        d_res_own,
        arrived,
        first,
        proj,
        edge,
        later,
        taps,
        h_mix,
        mixed_in,
        full,
        inverse_mix,
        gain_row,
    )
    d_proj, own, other, sent, gate_got, *pieces = tie(
        d_proj, own, other, sent, gate_got, *pieces
    )
    other = of_core(other)
    up_mine = add_dp(keep, pieces)
    sent, d_proj, up_mine, grad_taps, gain_dots, own, other, *pieces = tie(
        sent, d_proj, up_mine, grad_taps, gain_dots, own, other, *for_dp(own, other)
    )
    arrived, up_got, pieces = swap(sent, "y"), to_tok(up_mine), to_dp(pieces)
    near_sums = jnp.concatenate([grad_taps[0, :3], grad_taps[1, :3]], 1)
    sums = lax.dynamic_update_slice(jnp.zeros((3, features), F32), near_sums, (0, y * pair))
    gain_sum = gain_dots[:, 0] / mixer_norm_gain
    sums = jnp.concatenate([sums, gain_sum[None], grad_gain_ffn[None]], 0)
    sums = sum_over(sums, "c")
    if nx == 2:
        cross = [(2 * i + j, 2 * (1 - i) + 1 - j) for i in (0, 1) for j in (0, 1)]
        near, far = swap(sums, "y"), lax.ppermute(sums, ("dp", "y"), cross)
        sums = [sums, near, swap(sums, "dp"), far]
    else:
        sums = [sum_over(sum_over(sums, "dp"), "y")]
    [kept] = run_jobs(
        "back_in",
        scalars,
        [back_in_job(d_proj, first, full, inverse_mix, dots, gain_row, own_rows, F32)],
    )
    arrived, kept, up_got, sums, keep, *pieces = tie(
        arrived, kept, up_got, sums, for_self(own, other), *pieces
    )
    sums = (sums[0] + sums[1]) + (sums[2] + sums[3]) if nx == 2 else sums[0]
    mixer_mine = add_dp(keep, pieces)

    high = sums.astype(BF16)
    low = (sums - high.astype(F32)).astype(BF16)
    extra = jnp.concatenate([high, low, jnp.zeros((16 - 2 * sums.shape[0], features), BF16)], 0)
    mixer_mine = jnp.concatenate(
        [
            mixer_mine.reshape(nz, chunk, features),
            jnp.broadcast_to(extra, (nz, 16, features)),
        ],
        1,
    )
    mixer_got = to_tok(mixer_mine.reshape(nz * (chunk + 16), features))
    made_sent, arrived = tie(made_sent, arrived)
    made_arrived = swap(made_sent, "y")

    d_res_near = jnp.where(y == 0, d_res_full[:, :pair], d_res_full[:, pair:]).astype(F32)

    def by_core(value):
        mine = jnp.where(c == 0, value[:, :width], value[:, width:])
        theirs = jnp.where(c == 0, value[:, width:], value[:, :width])
        return by_rank(c, mine, swap(theirs, "c"))

    input_gradient = by_core(
        d_res_near + inverse_mix * (kept + arrived.astype(F32))
    )
    out_near = by_rank(
        y,
        (made_kept[:half] + made_arrived[half:].astype(F32)).astype(BF16),
        (made_kept[half:] + made_arrived[:half].astype(F32)).astype(BF16),
    )
    mixed = by_core(out_near)
    grad_down, grad_gate, grad_up = (add_tok(v) for v in (down_got, gate_got, up_got))
    mixer_sum = add_tok(mixer_got)
    grad_mixer = mixer_sum[:chunk]
    sums = mixer_sum[chunk : chunk + 5] + mixer_sum[chunk + 5 : chunk + 10]
    grad_in = grad_mixer[:, : 3 * width].reshape(chunk, 3, width)
    grad_out = grad_mixer[:, 3 * width :].T

    sums = lax.dynamic_slice_in_dim(sums, (2 * y + c) * width, width, 1)

    return (
        mixed,
        input_gradient,
        grad_in,
        sums[:3],
        grad_out,
        grad_gate,
        grad_up,
        grad_down.T,
        sums[3],
        sums[4],
    )


def solution(mesh):
    split = Mesh(
        mesh.devices.reshape(mesh.shape["dp"], mesh.shape["tok"], mesh.shape["mp"] // 2, 2),
        ("dp", "tok", "y", "c"),
    )
    tok, mp = ("dp", "tok"), ("y", "c")
    return jax.shard_map(
        body,
        mesh=split,
        in_specs=(
            P(tok, mp),
            P(tok, None, mp),
            P(None, mp),
            P(mp, tok),
            P(tok, mp),
            P(tok, mp),
            P(mp, tok),
            P(),
            P(),
            P(tok, mp),
        ),
        out_specs=(
            P(tok, mp),
            P(tok, mp),
            P(tok, None, mp),
            P(None, mp),
            P(mp, tok),
            P(tok, mp),
            P(tok, mp),
            P(mp, tok),
            P(mp),
            P(mp),
        ),
        check_vma=False,
    )
```

```python
import functools

import jax
import jax.numpy as jnp
from jax import lax
from jax.experimental import pallas as pl
from jax.experimental.layout import Layout, with_layout_constraint
from jax.experimental.pallas import tpu as pltpu
from jax.sharding import Mesh
from jax.sharding import PartitionSpec as P

EPS = 1e-05
F32 = jnp.float32
BF16 = jnp.bfloat16
VMEM_LIMIT = 56 * 2**20


def swap(value, axis):
    return lax.ppermute(value, axis, [(0, 1), (1, 0)])


def fetch(value, axis, distance):
    size = lax.axis_size(axis)
    return lax.ppermute(value, axis, [(s, (s - distance) % size) for s in range(size)])


def deliver(value, axis, distance):
    size = lax.axis_size(axis)
    return lax.ppermute(value, axis, [(s, (s + distance) % size) for s in range(size)])


def dot(left, right, contract):
    return lax.dot_general(left, right, (contract, ((), ())), preferred_element_type=F32)


def nn(left, right):
    return dot(left, right, ((1,), (0,)))


def nt(left, right):
    return dot(left, right, ((1,), (1,)))


def tn(left, right):
    return dot(left, right, ((0,), (0,)))


def total(values):
    result = values[0].astype(F32)
    for value in values[1:]:
        result = result + value.astype(F32)
    return result


def tie(*values):
    return lax.optimization_barrier(values)


def pick_rows(value, index, size):
    return lax.dynamic_slice_in_dim(value, index * size, size, 0)


def by_rank(index, first, second, axis=0):
    return jnp.where(
        index == 0,
        jnp.concatenate([first, second], axis),
        jnp.concatenate([second, first], axis),
    )


def for_dp(own, other):
    steps = lax.axis_size("dp")
    size = own.shape[0] // steps
    indices = [(lax.axis_index("dp") + i) % steps for i in range(1, steps)]
    return [
        total([pick_rows(part, index, size) for part in (own, other)]).astype(BF16)
        for index in indices
    ]


def to_dp(pieces):
    return [deliver(piece, "dp", i + 1) for i, piece in enumerate(pieces)]


def to_tok(mine):
    return lax.all_to_all(mine, "tok", split_axis=0, concat_axis=0, tiled=True)


def add_tok(got):
    steps = lax.axis_size("tok")
    size = got.shape[0] // steps
    return total([got[i * size : (i + 1) * size] for i in range(steps)])


def for_self(own, other):
    size = own.shape[0] // lax.axis_size("dp")
    mine = [pick_rows(part, lax.axis_index("dp"), size) for part in (own, other)]
    return total(mine).astype(BF16)


def add_dp(keep, arrived):
    return total([keep, *arrived]).astype(BF16)


def for_tok(parts, steps):
    count = lax.axis_size("tok")
    size = parts[0].shape[0] // count
    index = (lax.axis_index("tok") + steps) % count
    return total([pick_rows(part, index, size) for part in parts])


def sum_over(value, axis):
    size = lax.axis_size(axis)
    if size & (size - 1):
        return lax.psum(value, axis)
    step = 1
    while step < size:
        value = value + lax.ppermute(value, axis, [(s, s ^ step) for s in range(size)])
        step *= 2
    return value


def hidden_kernel(scalars, h_own, h_other, cot, w_gate, w_up, w_down, h, *outs):
    features = h.shape[1]
    half = h_own.shape[0]

    @pl.when(pl.program_id(0) == 0)
    def _():
        h[:half, :] = h_own[...]
        h[half:, :] = h_other[...]

    core = scalars[0]

    def both(w):
        return jnp.concatenate(
            [w[:, i].reshape(features, w.shape[3]) for i in (core, 1 - core)], 1
        )

    w_gate, w_up, w_down = both(w_gate), both(w_up), both(w_down)
    width = w_gate.shape[1] // 2
    step = 256
    for start in range(0, h.shape[0], step):
        part = pl.ds(start, step)
        gate, up = nn(h[part, :], w_gate), nn(h[part, :], w_up)
        d_hidden = nn(cot[part, :], w_down)
        sigma = jax.nn.sigmoid(gate)
        silu = gate * sigma
        results = (
            silu * up,
            d_hidden * up * sigma * (1.0 + gate * (1.0 - sigma)),
            d_hidden * silu,
        )
        for i, value in enumerate(results):
            value = value.astype(BF16)
            outs[2 * i][part, :] = value[:, :width]
            outs[2 * i + 1][part, :] = value[:, width:]


def hidden_units(scalars, h_own, h_other, cot, weights):
    rows, features = cot.shape
    blocks, _, chunk, width = weights.shape
    width //= 3
    tile = 128
    tiles = width // tile

    def of(matrix):
        return pl.BlockSpec((blocks, 2, chunk, tile), lambda j, s: (0, 0, 0, matrix * tiles + j))

    whole = pl.BlockSpec((rows, features), lambda j, s: (0, 0))
    half = pl.BlockSpec((rows // 2, features), lambda j, s: (0, 0))
    return pl.pallas_call(
        hidden_kernel,
        out_shape=[jax.ShapeDtypeStruct((rows, features), BF16)]
        + [jax.ShapeDtypeStruct((rows, width), BF16)] * 6,
        grid_spec=pltpu.PrefetchScalarGridSpec(
            num_scalar_prefetch=1,
            grid=(tiles,),
            in_specs=[half, half, whole, of(0), of(1), of(2)],
            out_specs=[whole] + [pl.BlockSpec((rows, tile), lambda j, s: (0, j))] * 6,
        ),
        compiler_params=pltpu.CompilerParams(vmem_limit_bytes=VMEM_LIMIT),
        name="hidden_units",
    )(scalars, h_own, h_other, cot, weights, weights, weights)


def run_jobs(name, scalars, jobs, limit=56):
    starts, steps = [], 0
    for job in jobs:
        starts.append(steps)
        steps += job[0]
    in_specs, out_specs, shapes, args, counts = [], [], [], [], []

    def spec(block, index, start, size):
        return pl.BlockSpec(block, lambda t, s: index(jnp.clip(t - start, 0, size - 1), s))

    for start, (size, inputs, outputs, _) in zip(starts, jobs):
        for array, block, index in inputs:
            in_specs.append(spec(block, index, start, size))
            args.append(array)
        for shape, dtype, block, index in outputs:
            out_specs.append(spec(block, index, start, size))
            shapes.append(jax.ShapeDtypeStruct(shape, dtype))
        counts.append((len(inputs), len(outputs)))

    def kernel(scalars_ref, *refs):
        ins, outs = list(refs[: len(in_specs)]), list(refs[len(in_specs) :])
        step = pl.program_id(0)
        for start, (size, _, _, work), (n_in, n_out) in zip(starts, jobs, counts):
            mine, ins = ins[:n_in], ins[n_in:]
            made, outs = outs[:n_out], outs[n_out:]
            if len(jobs) == 1:
                work(step, scalars_ref, mine, made)
            else:
                pl.when((step >= start) & (step < start + size))(
                    functools.partial(work, step - start, scalars_ref, mine, made)
                )

    return pl.pallas_call(
        kernel,
        out_shape=shapes,
        grid_spec=pltpu.PrefetchScalarGridSpec(
            num_scalar_prefetch=1, grid=(steps,), in_specs=in_specs, out_specs=out_specs
        ),
        compiler_params=pltpu.CompilerParams(vmem_limit_bytes=limit * 2**20),
        name=name,
    )(scalars, *args)


def sum_through(parts, weights, width):
    result = 0.0
    for part, weight in zip(parts, weights):
        for i in (0, 1):
            result = result + nt(part[i], weight[:, i].reshape(width, weight.shape[3]))
    return result


def sum_pairs(core, parts, weights, width):
    result = 0.0
    for i, weight in enumerate(weights):
        for part, index in ((parts[2 * i], core), (parts[2 * i + 1], 1 - core)):
            result = result + nt(part[...], weight[:, index].reshape(width, weight.shape[3]))
    return result


def hidden_back_job(pairs, weights, matrices, half):
    blocks, _, chunk, _ = weights.shape
    rows, width = pairs[0].shape
    rows //= 2
    features = blocks * chunk
    tile = max(256, chunk)
    inputs = [(part, (rows, width), lambda j, s: (half, 0)) for part in pairs] + [
        (weights, (tile // chunk, 2, chunk, width), lambda j, s, m=m: (j, 0, 0, m))
        for m in matrices
    ]
    count = len(pairs)

    def work(j, s, ins, outs):
        outs[0][...] = sum_pairs(s[0], ins[:count], ins[count:], tile).astype(BF16)

    outputs = [((rows, features), BF16, (rows, tile), lambda j, s: (0, j))]
    return features // tile, inputs, outputs, work


def back_job(parts, weights, matrices, rows_of, dtype, divide=1, block_of=None):
    blocks, _, chunk, _ = weights.shape
    _, rows, width = parts[0].shape
    features = blocks * chunk // divide
    tile = max(256, chunk)
    steps = features // tile
    if rows_of is not None:
        rows //= 2

    def at(j, s):
        return j if block_of is None else block_of(s) * steps + j

    inputs = [
        (part, (2, rows, width), lambda j, s: (0, 0 if rows_of is None else rows_of(s), 0))
        for part in parts
    ] + [
        (weights, (tile // chunk, 2, chunk, width), lambda j, s, m=m: (at(j, s), 0, 0, m))
        for m in matrices
    ]
    count = len(parts)

    def work(j, s, ins, outs):
        outs[0][...] = sum_through(ins[:count], ins[count:], tile).astype(dtype)

    return steps, inputs, [((rows, features), dtype, (rows, tile), lambda j, s: (0, j))], work


def back_tile(d_proj, weights, tokens, inverse, dots, gain, features):
    made = sum_through([d_proj], [weights], gain.shape[1]) * gain[...]
    scale = inverse[...] * (dots[0] + dots[1]) / features
    return made - tokens[...].astype(F32) * scale


def back_in_job(d_proj, weights, full, inverse, dots, gain, block_of, dtype):
    blocks, _, chunk, _ = weights.shape
    _, rows, width = d_proj.shape
    features = blocks * chunk
    tile = max(256, chunk)
    steps = features // tile // 2

    def at(j, s):
        return block_of(s) * steps + j

    inputs = [
        (d_proj, (2, rows, width), lambda j, s: (0, 0, 0)),
        (weights, (tile // chunk, 2, chunk, width), lambda j, s: (at(j, s), 0, 0, 0)),
        (full, (rows, tile), lambda j, s: (0, at(j, s))),
        (inverse, (rows, 1), lambda j, s: (0, 0)),
        (dots, (2, rows, 1), lambda j, s: (0, 0, 0)),
        (gain, (1, tile), lambda j, s: (0, at(j, s))),
    ]

    def work(j, s, ins, outs):
        outs[0][...] = back_tile(*ins, features).astype(dtype)

    outputs = [((rows, features // 2), dtype, (rows, tile), lambda j, s: (0, j))]
    return steps, inputs, outputs, work


def made_job(hidden, weights, matrix, residual):
    blocks, _, chunk, _ = weights.shape
    rows, width = hidden[0].shape
    features = blocks * chunk
    tile = max(256, chunk)
    steps = features // tile
    part = steps // 2
    height = residual.shape[0]

    def at(j, s):
        return jnp.where(j < part, (1 - s[1]) * part + j, s[1] * part + j - part)

    inputs = [(value, (rows, width), lambda j, s: (0, 0)) for value in hidden] + [
        (weights, (tile // chunk, 2, chunk, width), lambda j, s: (at(j, s), 0, 0, matrix)),
        (residual, (height, tile), lambda j, s: (0, at(j, s))),
    ]
    outputs = [
        ((rows, features // 2), BF16, (rows, tile), lambda j, s: (0, jnp.minimum(j, part - 1))),
        ((rows, features // 2), F32, (rows, tile), lambda j, s: (0, jnp.maximum(j - part, 0))),
    ]

    def work(j, s, ins, outs):
        result = sum_pairs(s[0], ins[:2], ins[2:3], tile)
        for out, mine in zip(outs, (j < part, j >= part)):

            @pl.when(mine)
            def _(out=out):
                out[:height, :] = (result[:height] + ins[3][...]).astype(out.dtype)
                out[height:, :] = result[height:].astype(out.dtype)

    return steps, inputs, outputs, work


def gradient_job(lefts, rights, devices):
    rows, features = lefts[0].shape
    width = rights[0].shape[1]
    size = features // devices
    tile = min(256, size)
    steps, mine = features // tile, size // tile
    inputs = [
        (left, (rows, tile), lambda j, s: (0, lax.rem(s[2] * mine + j, steps))) for left in lefts
    ] + [(right, (rows, width), lambda j, s: (0, 0)) for right in rights]
    outputs = [
        ((size, width), BF16, (tile, width), lambda j, s: (jnp.minimum(j, mine - 1), 0)),
        ((features - size, width), BF16, (tile, width), lambda j, s: (jnp.maximum(j - mine, 0), 0)),
    ]

    def work(j, s, ins, outs):
        made = (tn(ins[0][...], ins[2][...]) + tn(ins[1][...], ins[3][...])).astype(BF16)

        @pl.when(j < mine)
        def _():
            outs[0][...] = made

        @pl.when(j >= mine)
        def _():
            outs[1][...] = made

    return steps, inputs, outputs, work


def norm_job(full, gain):
    rows, features = full.shape
    tile = rows // 4

    def work(j, s, ins, outs):
        value = ins[0][...].astype(F32)
        inverse = lax.rsqrt(jnp.mean(value * value, -1, keepdims=True) + EPS)
        outs[0][...] = (value * inverse * ins[1][...]).astype(BF16)
        outs[1][...] = inverse

    inputs = [
        (full, (tile, features), lambda j, s: (j, 0)),
        (gain, (1, features), lambda j, s: (0, 0)),
    ]
    outputs = [
        ((rows, features), BF16, (tile, features), lambda j, s: (j, 0)),
        ((rows, 1), F32, (tile, 1), lambda j, s: (j, 0)),
    ]
    return 4, inputs, outputs, work


def tail_job(h, weights, width):
    rows, features = h.shape
    blocks, _, chunk, _ = weights.shape

    def work(j, s, ins, outs):
        b, xin = (nn(ins[0][...], w[:, 0].reshape(features, width)) for w in ins[1:])
        outs[0][0] = (b * xin).astype(BF16)

    inputs = [(h, (8, features), lambda j, s: (rows // 8 - 1, 0))] + [
        (weights, (blocks, 1, chunk, width), lambda j, s, k=k: (0, j, 0, k)) for k in (0, 2)
    ]
    return 2, inputs, [((2, 8, width), BF16, (1, 8, width), lambda j, s: (j, 0, 0))], work


def project_job(h, weights, width):
    rows, features = h.shape
    blocks, _, chunk, _ = weights.shape
    def work(j, s, ins, outs):
        outs[0][0] = nn(ins[0][...], ins[1][:, 0].reshape(features, width))

    inputs = [
        (h, (rows, features), lambda j, s: (0, 0)),
        (weights, (blocks, 1, chunk, width), lambda j, s: (0, j // 3, 0, j % 3)),
    ]
    block = (1, rows, width)
    outputs = [((2, rows, 3 * width), F32, block, lambda j, s: (j // 3, 0, j % 3))]
    return 6, inputs, outputs, work


def mix_job(proj, edge, taps, weights):
    _, rows, width = proj.shape
    width //= 3
    half = rows // 2
    blocks, _, chunk, _ = weights.shape
    features = blocks * chunk
    tile = 256

    def core(j):
        return jnp.minimum(j, 1)

    def later(j):
        return jnp.maximum(j - 2, 0)

    inputs = [
        (proj, (1, rows, 3 * width), lambda j, s: (core(j), 0, 0)),
        (edge, (1, 2, width), lambda j, s: (core(j), 0, 0)),
        (taps, (1, 3, width), lambda j, s: (core(j), 0, 0)),
        (weights, (tile // chunk, 2, chunk, width), lambda j, s: (later(j), 0, 0, 3)),
    ]
    outputs = [
        ((2, rows, width), BF16, (2, rows, width), lambda j, s: (0, 0, 0)),
        ((half, features), BF16, (half, tile), lambda j, s: (0, later(j))),
    ]

    def work(j, s, ins, outs):
        values, before, filters, weight = ins

        @pl.when(j < 2)
        def _():
            b, gate, xin = (values[0, :, i * width : (i + 1) * width] for i in range(3))
            gated = (b * xin).astype(BF16).astype(F32)
            arriving = before[0].astype(F32)
            back = [shifted(gated, arriving, 2), shifted(gated, arriving, 1), gated]
            conv = sum(filters[0, k : k + 1, :] * back[k] for k in range(3))
            outs[0][j] = (gate * conv).astype(BF16)

        @pl.when(j >= 2)
        def _():
            start = pl.multiple_of((1 - s[1]) * half, half)
            made = 0.0
            for i in (0, 1):
                part = outs[0][i, pl.ds(start, half), :]
                made = made + nt(part, weight[:, i].reshape(tile, width))
            outs[1][...] = made.astype(BF16)

    return 2 + features // tile, inputs, outputs, work


def shifted(value, edge, distance):
    rows = value.shape[0]
    at = lax.broadcasted_iota(jnp.int32, value.shape, 0)
    moved = pltpu.roll(value, distance % rows, 0)
    if distance > 0:
        for i in range(distance):
            moved = jnp.where(at == i, edge[2 - distance + i : 3 - distance + i, :], moved)
    else:
        for i in range(-distance):
            moved = jnp.where(at == rows + distance + i, edge[i : i + 1, :], moved)
    return moved


def mixer_back_kernel(
    scalars,
    own,
    arrived,
    w_out,
    proj,
    edge,
    later,
    taps,
    h,
    mixed,
    w_in,
    tokens,
    inverse,
    gain,
    full,
    d_proj,
    dots,
    sums,
    grad_own,
    grad_other,
    gain_dots,
    sent,
):
    half = own.shape[0]
    width = w_out.shape[3]
    step = pl.program_id(0)
    core, rank = scalars[0], scalars[1]

    @pl.when(step == 0)
    def _():
        full[pl.ds(pl.multiple_of(rank * half, half), half), :] = own[...]
        full[pl.ds(pl.multiple_of((1 - rank) * half, half), half), :] = arrived[...]

    @pl.when(step < 2)
    def _():
        weight = w_out[:, 0].reshape(full.shape[1], width)
        d_y = nn(full[...], weight)
        b, gate, xin = (proj[0, :, i * width : (i + 1) * width] for i in range(3))
        gated = (b * xin).astype(BF16).astype(F32)
        before = edge[0].astype(F32)
        back = [shifted(gated, before, 2), shifted(gated, before, 1), gated]
        conv = sum(taps[0, k : k + 1, :] * back[k] for k in range(3))
        d_conv = (d_y * gate).astype(BF16).astype(F32)
        following = later[0].astype(F32)
        d_gated = (
            taps[0, 2:3, :] * d_conv
            + taps[0, 1:2, :] * shifted(d_conv, following, -1)
            + taps[0, 0:1, :] * shifted(d_conv, following, -2)
        )
        parts = [(d_gated * xin).astype(BF16), (d_y * conv).astype(BF16), (d_gated * b).astype(BF16)]
        for i, part in enumerate(parts):
            d_proj[step, :, i * width : (i + 1) * width] = part
        product = sum(part.astype(F32) * gate for part, gate in zip(parts, (b, gate, xin)))
        dots[step] = jnp.sum(product, -1, keepdims=True)
        rows = [jnp.sum(d_conv * value, 0, keepdims=True) for value in back]
        sums[0] = jnp.concatenate(rows + [jnp.zeros((5, width), F32)], 0)

    tiles = full.shape[1] // grad_own.shape[0]

    @pl.when((step >= 2) & (step < 2 + tiles))
    def _():
        tile = grad_own.shape[0]
        start = pl.multiple_of((step - 2) * tile, tile)
        dot = 0.0
        for out, index in ((grad_own, core), (grad_other, 1 - core)):
            made = tn(h[...], d_proj[index])
            out[:, : 3 * width] = made.astype(BF16)
            weight = w_in[:, index].reshape(made.shape).astype(F32)
            dot = dot + jnp.sum(made * weight, -1, keepdims=True)
            out[:, 3 * width :] = tn(full[:, pl.ds(start, tile)], mixed[index]).astype(BF16)
        gain_dots[...] = jnp.broadcast_to(dot, gain_dots.shape)

    @pl.when(step >= 2 + tiles)
    def _():
        sent[...] = back_tile(d_proj, w_in, tokens, inverse, dots, gain, full.shape[1]).astype(BF16)


def mixer_back(
    scalars, own, arrived, weights, proj, edge, later, taps, h, mixed, tokens, inverse, gain
):
    half, features = own.shape
    rows = 2 * half
    blocks, _, chunk, _ = weights.shape
    width = proj.shape[2] // 3
    tile = 256

    def per_core(shape):
        return pl.BlockSpec((1, *shape), lambda t, s: (jnp.minimum(t, 1), 0, 0))

    def whole(shape):
        return pl.BlockSpec(shape, lambda t, s: (0,) * len(shape))

    tiles = features // tile

    def tiled(block):
        return pl.BlockSpec(
            block, lambda t, s: (jnp.clip(t - 2, 0, tiles - 1),) + (0,) * (len(block) - 1)
        )

    def back(t, s):
        return (1 - s[1]) * (tiles // 2) + jnp.maximum(t - 2 - tiles, 0)

    def of_tile(t, s):
        return jnp.where(t < 2 + tiles, jnp.maximum(t - 2, 0), back(t, s))

    return pl.pallas_call(
        mixer_back_kernel,
        out_shape=[
            jax.ShapeDtypeStruct((rows, features), BF16),
            jax.ShapeDtypeStruct((2, rows, 3 * width), BF16),
            jax.ShapeDtypeStruct((2, rows, 1), F32),
            jax.ShapeDtypeStruct((2, 8, width), F32),
            jax.ShapeDtypeStruct((features, 4 * width), BF16),
            jax.ShapeDtypeStruct((features, 4 * width), BF16),
            jax.ShapeDtypeStruct((features, 128), F32),
            jax.ShapeDtypeStruct((rows, features // 2), BF16),
        ],
        grid_spec=pltpu.PrefetchScalarGridSpec(
            num_scalar_prefetch=1,
            grid=(2 + tiles + tiles // 2,),
            in_specs=[
                whole((half, features)),
                whole((half, features)),
                pl.BlockSpec((blocks, 1, chunk, width), lambda t, s: (0, jnp.minimum(t, 1), 0, 3)),
                per_core((rows, 3 * width)),
                per_core((2, width)),
                per_core((2, width)),
                per_core((3, width)),
                pl.BlockSpec((rows, tile), lambda t, s: (0, jnp.clip(t - 2, 0, tiles - 1))),
                whole((2, rows, width)),
                pl.BlockSpec(
                    (tile // chunk, 2, chunk, 3 * width), lambda t, s: (of_tile(t, s), 0, 0, 0)
                ),
                pl.BlockSpec((rows, tile), lambda t, s: (0, back(t, s))),
                whole((rows, 1)),
                pl.BlockSpec((1, tile), lambda t, s: (0, back(t, s))),
            ],
            out_specs=[
                whole((rows, features)),
                whole((2, rows, 3 * width)),
                whole((2, rows, 1)),
                per_core((8, width)),
                tiled((tile, 4 * width)),
                tiled((tile, 4 * width)),
                tiled((tile, 128)),
                pl.BlockSpec((rows, tile), lambda t, s: (0, jnp.maximum(t - 2 - tiles, 0))),
            ],
        ),
        compiler_params=pltpu.CompilerParams(vmem_limit_bytes=VMEM_LIMIT),
        name="mixer_back",
    )(
        scalars, own, arrived, weights, proj, edge, later, taps, h, mixed, weights, tokens, inverse, gain
    )


def body(
    tokens,
    in_weight,
    conv_kernel,
    out_weight,
    gate_weight,
    up_weight,
    down_weight,
    mixer_norm_gain,
    gain_ffn,
    cotangent,
):
    x, z, y, c = (lax.axis_index(name) for name in ("dp", "tok", "y", "c"))
    nx, nz = lax.axis_size("dp"), lax.axis_size("tok")
    width = tokens.shape[1]
    features = 4 * width
    rows = tokens.shape[0] // 2
    half = rows // 2
    chunk = in_weight.shape[0]
    pair = 2 * width
    scalars = jnp.stack([c, y, x])
    gain_row = mixer_norm_gain[None]

    def to_mp(value):
        mine, theirs = pick_rows(value, c, rows), pick_rows(value, 1 - c, rows)
        cross = [(2 * i + j, 2 * (1 - i) + 1 - j) for i in (0, 1) for j in (0, 1)]
        return mine, swap(theirs, "c"), swap(mine, "y"), lax.ppermute(theirs, ("y", "c"), cross)

    def join_mp(mine, beside, across, cross):
        near = by_rank(c, mine, beside, 1)
        return near, by_rank(y, near, by_rank(c, across, cross, 1), 1)

    every = ("dp", "tok", "c")

    def gather(shard):
        shard = with_layout_constraint(shard, Layout((0, 1)))
        whole = lax.all_gather(shard, every, axis=0, tiled=True)
        return whole.reshape(features // chunk, 2, chunk, shard.shape[1])

    first = jnp.concatenate([in_weight.reshape(chunk, 3 * width), out_weight.T], 1)
    first = with_layout_constraint(first, Layout((0, 1)))
    blocks = [first] + [fetch(first, "tok", i) for i in range(1, nz)]
    weights = jnp.concatenate([gate_weight, up_weight, down_weight.T], 1)
    pieces = to_mp(tokens)
    weights, cotangent, *pieces = tie(weights, cotangent, *pieces, *blocks)
    pieces, blocks = pieces[:-nz], pieces[-nz:]
    weights = gather(weights)
    first_tok = lax.dynamic_slice_in_dim(
        jnp.concatenate(blocks + blocks[:-1], 0), ((nz - z) % nz) * chunk, nz * chunk
    )
    pieces_cot = to_mp(cotangent)
    taps = by_rank(c, conv_kernel[None], swap(conv_kernel, "c")[None]).astype(F32)

    def both_cores(part):
        mine, theirs = (v.reshape(-1, 1, chunk, v.shape[1]) for v in (part, swap(part, "c")))
        return by_rank(c, mine, theirs, 1)

    if nx == 2:
        first_dp = swap(first_tok, "dp")
        first_tok = both_cores(first_tok)
    else:
        first = lax.all_gather(both_cores(first_tok), "dp", axis=0, tiled=True)

    _, full = join_mp(*pieces)
    h_mix, inverse_mix = run_jobs("norm", scalars, [norm_job(full, gain_row)], 12)
    if nx == 2:
        first_dp, first_tok, h_mix, *pieces_cot = tie(first_dp, first_tok, h_mix, *pieces_cot)
        first = by_rank(x, first_tok, both_cores(first_dp))
    _, cot = join_mp(*pieces_cot)
    cot = jnp.concatenate([pick_rows(cot, y, half), pick_rows(cot, 1 - y, half)], 0)
    cot, cot_beside = tie(cot, swap(cot, "c"))

    ranks = nz * 2
    [gated] = run_jobs("tail", scalars, [tail_job(h_mix, first, width)], 16)
    edge = lax.ppermute(gated[:, -2:], ("tok", "c"), [(i, i + 1) for i in range(ranks - 1)])
    [proj] = run_jobs("project", scalars, [project_job(h_mix, first, width)], 20)
    gate_c = proj[:, :8, width : 2 * width]
    edge, proj = tie(edge, proj)
    mixed_in, sent = run_jobs("mix", scalars, [mix_job(proj, edge, taps, first)], 28)

    def own_rows(s):
        return s[1]

    def other_rows(s):
        return 1 - s[1]

    arrived = swap(sent, "y")
    [kept] = run_jobs(
        "project_out", scalars, [back_job((mixed_in,), first, (3,), own_rows, F32)], 20
    )
    w_out = [first[:, i, :, 3 * width :].reshape(features, width) for i in (0, 1)]
    arrived, kept, *w_out = tie(arrived, kept, *w_out)
    residual = pick_rows(full, y, half).astype(F32) + kept + arrived.astype(F32)

    inverse_ffn = lax.rsqrt(jnp.mean(residual * residual, -1, keepdims=True) + EPS)
    normalized = residual * inverse_ffn
    h_own = (normalized * gain_ffn).astype(BF16)
    h, *units = hidden_units(scalars, h_own, swap(h_own, "y"), cot, weights)
    hidden, d_gate, d_up = units[:2], units[2:4], units[4:]

    def of_core(other):
        return swap(other, "c")

    def pieces_of(send):
        size = features // nx
        return to_dp([send[i * size : (i + 1) * size] for i in range(nx - 1)])

    hidden_beside, h_beside = of_core(hidden[1]), of_core(h)
    [sent] = run_jobs(
        "back_hidden", scalars, [hidden_back_job([*d_gate, *d_up], weights, (0, 1), 1)]
    )
    sent, hidden_beside, h_beside, *units = tie(sent, hidden_beside, h_beside, *hidden, *d_gate, *d_up)
    hidden, d_gate, d_up = units[:2], units[2:4], units[4:]
    gate_beside, up_beside = of_core(d_gate[1]), of_core(d_up[1])
    keep, send = run_jobs(
        "down_gradient",
        scalars,
        [gradient_job([cot, cot_beside], [hidden[0], hidden_beside], nx)],
    )
    sent, keep, send, gate_beside, up_beside, *units = tie(
        sent, keep, send, gate_beside, up_beside, *hidden, *d_gate, *d_up
    )
    hidden, d_gate, d_up = units[:2], units[2:4], units[4:]
    arrived, pieces = swap(sent, "y"), pieces_of(send)
    next_keep, send, kept = run_jobs(
        "gate_gradient",
        scalars,
        [
            gradient_job([h, h_beside], [d_gate[0], gate_beside], nx),
            hidden_back_job([*d_gate, *d_up], weights, (0, 1), 0),
        ],
    )
    arrived, send, kept, *pieces = tie(arrived, send, kept, *pieces)
    d_h = kept.astype(F32) + arrived.astype(F32)
    grad_gain_ffn = jnp.sum(d_h * normalized, 0)
    scaled = d_h * gain_ffn
    d_res = cot[:half].astype(F32) + inverse_ffn * (
        scaled - normalized * jnp.mean(scaled * normalized, -1, keepdims=True)
    )
    d_res_own = d_res.astype(BF16)
    down_parts = [keep, *pieces]
    down_mine = [for_tok(down_parts, i).astype(BF16) for i in range(1, nz)]
    d_res_own, send, *units = tie(d_res_own, send, *hidden, *d_up, *down_mine)
    hidden, d_up, down_mine = units[:2], units[2:4], units[4:]
    arrived, pieces = swap(d_res_own, "y"), pieces_of(send)
    down_got = [deliver(part, "tok", i + 1) for i, part in enumerate(down_mine)]
    keep, send, made_sent, made_kept = run_jobs(
        "up_gradient",
        scalars,
        [
            gradient_job([h, h_beside], [d_up[0], up_beside], nx),
            made_job(hidden, weights, 2, residual),
        ],
    )
    arrived, send, made_sent, made_kept, *pieces = tie(
        arrived, send, made_sent, made_kept, *pieces, *down_got
    )
    pieces, down_got = pieces[: 1 - nz], pieces[1 - nz :]
    grad_down = total([for_tok(down_parts, 0), *down_got])
    gate_parts = [next_keep, *pieces]
    gate_mine = [for_tok(gate_parts, i).astype(BF16) for i in range(1, nz)]

    head = jnp.where(y == 0, d_res_own[:8], arrived[:8])
    d_head = jnp.stack([nn(head, w) for w in w_out])
    d_head = (d_head * gate_c).astype(BF16)[:, :2]
    later = lax.ppermute(d_head, ("tok", "c"), [(i + 1, i) for i in range(ranks - 1)])
    arrived, later, send, *gate_mine = tie(arrived, later, send, *gate_mine)
    pieces = pieces_of(send)
    gate_got = [deliver(part, "tok", i + 1) for i, part in enumerate(gate_mine)]
    d_res_full, d_proj, dots, grad_taps, own, other, gain_dots, sent = mixer_back(
        scalars,
        d_res_own,
        arrived,
        first,
        proj,
        edge,
        later,
        taps,
        h_mix,
        mixed_in,
        full,
        inverse_mix,
        gain_row,
    )
    d_proj, own, other, sent, *pieces = tie(d_proj, own, other, sent, *pieces, *gate_got)
    pieces, gate_got = pieces[: 1 - nz], pieces[1 - nz :]
    grad_gate = total([for_tok(gate_parts, 0), *gate_got])
    other = of_core(other)
    up_mine = add_dp(keep, pieces)
    sent, d_proj, up_mine, grad_taps, gain_dots, own, other, *pieces = tie(
        sent, d_proj, up_mine, grad_taps, gain_dots, own, other, *for_dp(own, other)
    )
    arrived, up_got, pieces = swap(sent, "y"), to_tok(up_mine), to_dp(pieces)
    near_sums = jnp.concatenate([grad_taps[0, :3], grad_taps[1, :3]], 1)
    sums = lax.dynamic_update_slice(jnp.zeros((3, features), F32), near_sums, (0, y * pair))
    gain_sum = gain_dots[:, 0] / mixer_norm_gain
    sums = jnp.concatenate([sums, gain_sum[None], grad_gain_ffn[None]], 0)
    sums = sum_over(sums, "c")
    if nx == 2:
        cross = [(2 * i + j, 2 * (1 - i) + 1 - j) for i in (0, 1) for j in (0, 1)]
        near, far = swap(sums, "y"), lax.ppermute(sums, ("dp", "y"), cross)
        sums = [sums, near, swap(sums, "dp"), far]
    else:
        sums = [sum_over(sum_over(sums, "dp"), "y")]
    [kept] = run_jobs(
        "back_in",
        scalars,
        [back_in_job(d_proj, first, full, inverse_mix, dots, gain_row, own_rows, F32)],
    )
    arrived, kept, up_got, sums, keep, *pieces = tie(
        arrived, kept, up_got, sums, for_self(own, other), *pieces
    )
    sums = (sums[0] + sums[1]) + (sums[2] + sums[3]) if nx == 2 else sums[0]
    mixer_mine = add_dp(keep, pieces)

    high = sums.astype(BF16)
    low = (sums - high.astype(F32)).astype(BF16)
    extra = jnp.concatenate([high, low, jnp.zeros((16 - 2 * sums.shape[0], features), BF16)], 0)
    mixer_mine = jnp.concatenate(
        [
            mixer_mine.reshape(nz, chunk, features),
            jnp.broadcast_to(extra, (nz, 16, features)),
        ],
        1,
    )
    mixer_got = to_tok(mixer_mine.reshape(nz * (chunk + 16), features))
    made_sent, arrived = tie(made_sent, arrived)
    made_arrived = swap(made_sent, "y")

    d_res_near = jnp.where(y == 0, d_res_full[:, :pair], d_res_full[:, pair:]).astype(F32)

    def by_core(value):
        mine = jnp.where(c == 0, value[:, :width], value[:, width:])
        theirs = jnp.where(c == 0, value[:, width:], value[:, :width])
        return by_rank(c, mine, swap(theirs, "c"))

    input_gradient = by_core(
        d_res_near + inverse_mix * (kept + arrived.astype(F32))
    )
    out_near = by_rank(
        y,
        (made_kept[:half] + made_arrived[half:].astype(F32)).astype(BF16),
        (made_kept[half:] + made_arrived[:half].astype(F32)).astype(BF16),
    )
    mixed = by_core(out_near)
    grad_up = add_tok(up_got)
    mixer_sum = add_tok(mixer_got)
    grad_mixer = mixer_sum[:chunk]
    sums = mixer_sum[chunk : chunk + 5] + mixer_sum[chunk + 5 : chunk + 10]
    grad_in = grad_mixer[:, : 3 * width].reshape(chunk, 3, width)
    grad_out = grad_mixer[:, 3 * width :].T

    sums = lax.dynamic_slice_in_dim(sums, (2 * y + c) * width, width, 1)

    return (
        mixed,
        input_gradient,
        grad_in,
        sums[:3],
        grad_out,
        grad_gate,
        grad_up,
        grad_down.T,
        sums[3],
        sums[4],
    )


def solution(mesh):
    split = Mesh(
        mesh.devices.reshape(mesh.shape["dp"], mesh.shape["tok"], mesh.shape["mp"] // 2, 2),
        ("dp", "tok", "y", "c"),
    )
    tok, mp = ("dp", "tok"), ("y", "c")
    return jax.shard_map(
        body,
        mesh=split,
        in_specs=(
            P(tok, mp),
            P(tok, None, mp),
            P(None, mp),
            P(mp, tok),
            P(tok, mp),
            P(tok, mp),
            P(mp, tok),
            P(),
            P(),
            P(tok, mp),
        ),
        out_specs=(
            P(tok, mp),
            P(tok, mp),
            P(tok, None, mp),
            P(None, mp),
            P(mp, tok),
            P(tok, mp),
            P(tok, mp),
            P(mp, tok),
            P(mp),
            P(mp),
        ),
        check_vma=False,
    )
```

```python
import functools

import jax
import jax.numpy as jnp
from jax import lax
from jax.experimental import pallas as pl
from jax.experimental.layout import Layout, with_layout_constraint
from jax.experimental.pallas import tpu as pltpu
from jax.sharding import Mesh
from jax.sharding import PartitionSpec as P

EPS = 1e-05
F32 = jnp.float32
BF16 = jnp.bfloat16
VMEM_LIMIT = 56 * 2**20


def swap(value, axis):
    return lax.ppermute(value, axis, [(0, 1), (1, 0)])


def fetch(value, axis, distance):
    size = lax.axis_size(axis)
    return lax.ppermute(value, axis, [(s, (s - distance) % size) for s in range(size)])


def deliver(value, axis, distance):
    size = lax.axis_size(axis)
    return lax.ppermute(value, axis, [(s, (s + distance) % size) for s in range(size)])


def dot(left, right, contract):
    return lax.dot_general(left, right, (contract, ((), ())), preferred_element_type=F32)


def nn(left, right):
    return dot(left, right, ((1,), (0,)))


def nt(left, right):
    return dot(left, right, ((1,), (1,)))


def tn(left, right):
    return dot(left, right, ((0,), (0,)))


def total(values):
    result = values[0].astype(F32)
    for value in values[1:]:
        result = result + value.astype(F32)
    return result


def tie(*values):
    return lax.optimization_barrier(values)


def pick_rows(value, index, size):
    return lax.dynamic_slice_in_dim(value, index * size, size, 0)


def by_rank(index, first, second, axis=0):
    return jnp.where(
        index == 0,
        jnp.concatenate([first, second], axis),
        jnp.concatenate([second, first], axis),
    )


def for_dp(own, other):
    steps = lax.axis_size("dp")
    size = own.shape[0] // steps
    indices = [(lax.axis_index("dp") + i) % steps for i in range(1, steps)]
    return [
        total([pick_rows(part, index, size) for part in (own, other)]).astype(BF16)
        for index in indices
    ]


def to_dp(pieces):
    return [deliver(piece, "dp", i + 1) for i, piece in enumerate(pieces)]


def to_tok(mine):
    return lax.all_to_all(mine, "tok", split_axis=0, concat_axis=0, tiled=True)


def add_tok(got):
    steps = lax.axis_size("tok")
    size = got.shape[0] // steps
    return total([got[i * size : (i + 1) * size] for i in range(steps)])


def for_self(own, other):
    size = own.shape[0] // lax.axis_size("dp")
    mine = [pick_rows(part, lax.axis_index("dp"), size) for part in (own, other)]
    return total(mine).astype(BF16)


def add_dp(keep, arrived):
    return total([keep, *arrived]).astype(BF16)


def for_tok(parts, steps):
    count = lax.axis_size("tok")
    size = parts[0].shape[0] // count
    index = (lax.axis_index("tok") + steps) % count
    return total([pick_rows(part, index, size) for part in parts])


def sum_over(value, axis):
    size = lax.axis_size(axis)
    if size & (size - 1):
        return lax.psum(value, axis)
    step = 1
    while step < size:
        value = value + lax.ppermute(value, axis, [(s, s ^ step) for s in range(size)])
        step *= 2
    return value


def hidden_kernel(scalars, h_own, h_other, cot, w_gate, w_up, w_down, h, *outs):
    features = h.shape[1]
    half = h_own.shape[0]

    @pl.when(pl.program_id(0) == 0)
    def _():
        h[:half, :] = h_own[...]
        h[half:, :] = h_other[...]

    core = scalars[0]

    def both(w):
        return jnp.concatenate(
            [w[:, i].reshape(features, w.shape[3]) for i in (core, 1 - core)], 1
        )

    w_gate, w_up, w_down = both(w_gate), both(w_up), both(w_down)
    width = w_gate.shape[1] // 2
    step = 256
    for start in range(0, h.shape[0], step):
        part = pl.ds(start, step)
        gate, up = nn(h[part, :], w_gate), nn(h[part, :], w_up)
        d_hidden = nn(cot[part, :], w_down)
        sigma = jax.nn.sigmoid(gate)
        silu = gate * sigma
        results = (
            silu * up,
            d_hidden * up * sigma * (1.0 + gate * (1.0 - sigma)),
            d_hidden * silu,
        )
        for i, value in enumerate(results):
            value = value.astype(BF16)
            outs[2 * i][part, :] = value[:, :width]
            outs[2 * i + 1][part, :] = value[:, width:]


def hidden_units(scalars, h_own, h_other, cot, weights):
    rows, features = cot.shape
    blocks, _, chunk, width = weights.shape
    width //= 3
    tile = 128
    tiles = width // tile

    def of(matrix):
        return pl.BlockSpec((blocks, 2, chunk, tile), lambda j, s: (0, 0, 0, matrix * tiles + j))

    whole = pl.BlockSpec((rows, features), lambda j, s: (0, 0))
    half = pl.BlockSpec((rows // 2, features), lambda j, s: (0, 0))
    return pl.pallas_call(
        hidden_kernel,
        out_shape=[jax.ShapeDtypeStruct((rows, features), BF16)]
        + [jax.ShapeDtypeStruct((rows, width), BF16)] * 6,
        grid_spec=pltpu.PrefetchScalarGridSpec(
            num_scalar_prefetch=1,
            grid=(tiles,),
            in_specs=[half, half, whole, of(0), of(1), of(2)],
            out_specs=[whole] + [pl.BlockSpec((rows, tile), lambda j, s: (0, j))] * 6,
        ),
        compiler_params=pltpu.CompilerParams(vmem_limit_bytes=VMEM_LIMIT),
        name="hidden_units",
    )(scalars, h_own, h_other, cot, weights, weights, weights)


def run_jobs(name, scalars, jobs, limit=56):
    starts, steps = [], 0
    for job in jobs:
        starts.append(steps)
        steps += job[0]
    in_specs, out_specs, shapes, args, counts = [], [], [], [], []

    def spec(block, index, start, size):
        return pl.BlockSpec(block, lambda t, s: index(jnp.clip(t - start, 0, size - 1), s))

    for start, (size, inputs, outputs, _) in zip(starts, jobs):
        for array, block, index in inputs:
            in_specs.append(spec(block, index, start, size))
            args.append(array)
        for shape, dtype, block, index in outputs:
            out_specs.append(spec(block, index, start, size))
            shapes.append(jax.ShapeDtypeStruct(shape, dtype))
        counts.append((len(inputs), len(outputs)))

    def kernel(scalars_ref, *refs):
        ins, outs = list(refs[: len(in_specs)]), list(refs[len(in_specs) :])
        step = pl.program_id(0)
        for start, (size, _, _, work), (n_in, n_out) in zip(starts, jobs, counts):
            mine, ins = ins[:n_in], ins[n_in:]
            made, outs = outs[:n_out], outs[n_out:]
            if len(jobs) == 1:
                work(step, scalars_ref, mine, made)
            else:
                pl.when((step >= start) & (step < start + size))(
                    functools.partial(work, step - start, scalars_ref, mine, made)
                )

    return pl.pallas_call(
        kernel,
        out_shape=shapes,
        grid_spec=pltpu.PrefetchScalarGridSpec(
            num_scalar_prefetch=1, grid=(steps,), in_specs=in_specs, out_specs=out_specs
        ),
        compiler_params=pltpu.CompilerParams(vmem_limit_bytes=limit * 2**20),
        name=name,
    )(scalars, *args)


def sum_through(parts, weights, width):
    result = 0.0
    for part, weight in zip(parts, weights):
        for i in (0, 1):
            result = result + nt(part[i], weight[:, i].reshape(width, weight.shape[3]))
    return result


def sum_pairs(core, parts, weights, width):
    result = 0.0
    for i, weight in enumerate(weights):
        for part, index in ((parts[2 * i], core), (parts[2 * i + 1], 1 - core)):
            result = result + nt(part[...], weight[:, index].reshape(width, weight.shape[3]))
    return result


def hidden_back_job(pairs, weights, matrices, half):
    blocks, _, chunk, _ = weights.shape
    rows, width = pairs[0].shape
    rows //= 2
    features = blocks * chunk
    tile = max(256, chunk)
    inputs = [(part, (rows, width), lambda j, s: (half, 0)) for part in pairs] + [
        (weights, (tile // chunk, 2, chunk, width), lambda j, s, m=m: (j, 0, 0, m))
        for m in matrices
    ]
    count = len(pairs)

    def work(j, s, ins, outs):
        outs[0][...] = sum_pairs(s[0], ins[:count], ins[count:], tile).astype(BF16)

    outputs = [((rows, features), BF16, (rows, tile), lambda j, s: (0, j))]
    return features // tile, inputs, outputs, work


def back_job(parts, weights, matrices, rows_of, dtype, divide=1, block_of=None):
    blocks, _, chunk, _ = weights.shape
    _, rows, width = parts[0].shape
    features = blocks * chunk // divide
    tile = max(256, chunk)
    steps = features // tile
    if rows_of is not None:
        rows //= 2

    def at(j, s):
        return j if block_of is None else block_of(s) * steps + j

    inputs = [
        (part, (2, rows, width), lambda j, s: (0, 0 if rows_of is None else rows_of(s), 0))
        for part in parts
    ] + [
        (weights, (tile // chunk, 2, chunk, width), lambda j, s, m=m: (at(j, s), 0, 0, m))
        for m in matrices
    ]
    count = len(parts)

    def work(j, s, ins, outs):
        outs[0][...] = sum_through(ins[:count], ins[count:], tile).astype(dtype)

    return steps, inputs, [((rows, features), dtype, (rows, tile), lambda j, s: (0, j))], work


def back_tile(d_proj, weights, tokens, inverse, dots, gain, features):
    made = sum_through([d_proj], [weights], gain.shape[1]) * gain[...]
    scale = inverse[...] * (dots[0] + dots[1]) / features
    return made - tokens[...].astype(F32) * scale


def back_in_job(d_proj, weights, full, inverse, dots, gain, block_of, dtype):
    blocks, _, chunk, _ = weights.shape
    _, rows, width = d_proj.shape
    features = blocks * chunk
    tile = max(256, chunk)
    steps = features // tile // 2

    def at(j, s):
        return block_of(s) * steps + j

    inputs = [
        (d_proj, (2, rows, width), lambda j, s: (0, 0, 0)),
        (weights, (tile // chunk, 2, chunk, width), lambda j, s: (at(j, s), 0, 0, 0)),
        (full, (rows, tile), lambda j, s: (0, at(j, s))),
        (inverse, (rows, 1), lambda j, s: (0, 0)),
        (dots, (2, rows, 1), lambda j, s: (0, 0, 0)),
        (gain, (1, tile), lambda j, s: (0, at(j, s))),
    ]

    def work(j, s, ins, outs):
        outs[0][...] = back_tile(*ins, features).astype(dtype)

    outputs = [((rows, features // 2), dtype, (rows, tile), lambda j, s: (0, j))]
    return steps, inputs, outputs, work


def made_job(hidden, weights, matrix, residual):
    blocks, _, chunk, _ = weights.shape
    rows, width = hidden[0].shape
    features = blocks * chunk
    tile = max(256, chunk)
    steps = features // tile
    part = steps // 2
    height = residual.shape[0]

    def at(j, s):
        return jnp.where(j < part, (1 - s[1]) * part + j, s[1] * part + j - part)

    inputs = [(value, (rows, width), lambda j, s: (0, 0)) for value in hidden] + [
        (weights, (tile // chunk, 2, chunk, width), lambda j, s: (at(j, s), 0, 0, matrix)),
        (residual, (height, tile), lambda j, s: (0, at(j, s))),
    ]
    outputs = [
        ((rows, features // 2), BF16, (rows, tile), lambda j, s: (0, jnp.minimum(j, part - 1))),
        ((rows, features // 2), F32, (rows, tile), lambda j, s: (0, jnp.maximum(j - part, 0))),
    ]

    def work(j, s, ins, outs):
        result = sum_pairs(s[0], ins[:2], ins[2:3], tile)
        for out, mine in zip(outs, (j < part, j >= part)):

            @pl.when(mine)
            def _(out=out):
                out[:height, :] = (result[:height] + ins[3][...]).astype(out.dtype)
                out[height:, :] = result[height:].astype(out.dtype)

    return steps, inputs, outputs, work


def gradient_job(lefts, rights, devices):
    rows, features = lefts[0].shape
    width = rights[0].shape[1]
    size = features // devices
    tile = min(256, size)
    steps, mine = features // tile, size // tile
    inputs = [
        (left, (rows, tile), lambda j, s: (0, lax.rem(s[2] * mine + j, steps))) for left in lefts
    ] + [(right, (rows, width), lambda j, s: (0, 0)) for right in rights]
    outputs = [
        ((size, width), BF16, (tile, width), lambda j, s: (jnp.minimum(j, mine - 1), 0)),
        ((features - size, width), BF16, (tile, width), lambda j, s: (jnp.maximum(j - mine, 0), 0)),
    ]

    def work(j, s, ins, outs):
        made = (tn(ins[0][...], ins[2][...]) + tn(ins[1][...], ins[3][...])).astype(BF16)

        @pl.when(j < mine)
        def _():
            outs[0][...] = made

        @pl.when(j >= mine)
        def _():
            outs[1][...] = made

    return steps, inputs, outputs, work


def norm_job(full, gain):
    rows, features = full.shape
    tile = rows // 4

    def work(j, s, ins, outs):
        value = ins[0][...].astype(F32)
        inverse = lax.rsqrt(jnp.mean(value * value, -1, keepdims=True) + EPS)
        outs[0][...] = (value * inverse * ins[1][...]).astype(BF16)
        outs[1][...] = inverse

    inputs = [
        (full, (tile, features), lambda j, s: (j, 0)),
        (gain, (1, features), lambda j, s: (0, 0)),
    ]
    outputs = [
        ((rows, features), BF16, (tile, features), lambda j, s: (j, 0)),
        ((rows, 1), F32, (tile, 1), lambda j, s: (j, 0)),
    ]
    return 4, inputs, outputs, work


def tail_job(h, weights, width):
    rows, features = h.shape
    blocks, _, chunk, _ = weights.shape

    def work(j, s, ins, outs):
        b, xin = (nn(ins[0][...], w[:, 0].reshape(features, width)) for w in ins[1:])
        outs[0][0] = (b * xin).astype(BF16)

    inputs = [(h, (8, features), lambda j, s: (rows // 8 - 1, 0))] + [
        (weights, (blocks, 1, chunk, width), lambda j, s, k=k: (0, j, 0, k)) for k in (0, 2)
    ]
    return 2, inputs, [((2, 8, width), BF16, (1, 8, width), lambda j, s: (j, 0, 0))], work


def project_job(h, weights, width):
    rows, features = h.shape
    blocks, _, chunk, _ = weights.shape
    def work(j, s, ins, outs):
        outs[0][0] = nn(ins[0][...], ins[1][:, 0].reshape(features, width))

    inputs = [
        (h, (rows, features), lambda j, s: (0, 0)),
        (weights, (blocks, 1, chunk, width), lambda j, s: (0, j // 3, 0, j % 3)),
    ]
    block = (1, rows, width)
    outputs = [((2, rows, 3 * width), F32, block, lambda j, s: (j // 3, 0, j % 3))]
    return 6, inputs, outputs, work


def mix_job(proj, edge, taps, weights):
    _, rows, width = proj.shape
    width //= 3
    half = rows // 2
    blocks, _, chunk, _ = weights.shape
    features = blocks * chunk
    tile = 256

    def core(j):
        return jnp.minimum(j, 1)

    def later(j):
        return jnp.maximum(j - 2, 0)

    inputs = [
        (proj, (1, rows, 3 * width), lambda j, s: (core(j), 0, 0)),
        (edge, (1, 2, width), lambda j, s: (core(j), 0, 0)),
        (taps, (1, 3, width), lambda j, s: (core(j), 0, 0)),
        (weights, (tile // chunk, 2, chunk, width), lambda j, s: (later(j), 0, 0, 3)),
    ]
    outputs = [
        ((2, rows, width), BF16, (2, rows, width), lambda j, s: (0, 0, 0)),
        ((half, features), BF16, (half, tile), lambda j, s: (0, later(j))),
    ]

    def work(j, s, ins, outs):
        values, before, filters, weight = ins

        @pl.when(j < 2)
        def _():
            b, gate, xin = (values[0, :, i * width : (i + 1) * width] for i in range(3))
            gated = (b * xin).astype(BF16).astype(F32)
            arriving = before[0].astype(F32)
            back = [shifted(gated, arriving, 2), shifted(gated, arriving, 1), gated]
            conv = sum(filters[0, k : k + 1, :] * back[k] for k in range(3))
            outs[0][j] = (gate * conv).astype(BF16)

        @pl.when(j >= 2)
        def _():
            start = pl.multiple_of((1 - s[1]) * half, half)
            made = 0.0
            for i in (0, 1):
                part = outs[0][i, pl.ds(start, half), :]
                made = made + nt(part, weight[:, i].reshape(tile, width))
            outs[1][...] = made.astype(BF16)

    return 2 + features // tile, inputs, outputs, work


def shifted(value, edge, distance):
    rows = value.shape[0]
    at = lax.broadcasted_iota(jnp.int32, value.shape, 0)
    moved = pltpu.roll(value, distance % rows, 0)
    if distance > 0:
        for i in range(distance):
            moved = jnp.where(at == i, edge[2 - distance + i : 3 - distance + i, :], moved)
    else:
        for i in range(-distance):
            moved = jnp.where(at == rows + distance + i, edge[i : i + 1, :], moved)
    return moved


def mixer_back_kernel(
    scalars,
    own,
    arrived,
    w_out,
    proj,
    edge,
    later,
    taps,
    h,
    mixed,
    w_in,
    tokens,
    inverse,
    gain,
    full,
    d_proj,
    dots,
    sums,
    grad_own,
    grad_other,
    gain_dots,
    sent,
):
    half = own.shape[0]
    width = w_out.shape[3]
    step = pl.program_id(0)
    core, rank = scalars[0], scalars[1]

    @pl.when(step == 0)
    def _():
        full[pl.ds(pl.multiple_of(rank * half, half), half), :] = own[...]
        full[pl.ds(pl.multiple_of((1 - rank) * half, half), half), :] = arrived[...]

    @pl.when(step < 2)
    def _():
        weight = w_out[:, 0].reshape(full.shape[1], width)
        d_y = nn(full[...], weight)
        b, gate, xin = (proj[0, :, i * width : (i + 1) * width] for i in range(3))
        gated = (b * xin).astype(BF16).astype(F32)
        before = edge[0].astype(F32)
        back = [shifted(gated, before, 2), shifted(gated, before, 1), gated]
        conv = sum(taps[0, k : k + 1, :] * back[k] for k in range(3))
        d_conv = (d_y * gate).astype(BF16).astype(F32)
        following = later[0].astype(F32)
        d_gated = (
            taps[0, 2:3, :] * d_conv
            + taps[0, 1:2, :] * shifted(d_conv, following, -1)
            + taps[0, 0:1, :] * shifted(d_conv, following, -2)
        )
        parts = [(d_gated * xin).astype(BF16), (d_y * conv).astype(BF16), (d_gated * b).astype(BF16)]
        for i, part in enumerate(parts):
            d_proj[step, :, i * width : (i + 1) * width] = part
        product = sum(part.astype(F32) * gate for part, gate in zip(parts, (b, gate, xin)))
        dots[step] = jnp.sum(product, -1, keepdims=True)
        rows = [jnp.sum(d_conv * value, 0, keepdims=True) for value in back]
        sums[0] = jnp.concatenate(rows + [jnp.zeros((5, width), F32)], 0)

    tiles = full.shape[1] // grad_own.shape[0]

    @pl.when((step >= 2) & (step < 2 + tiles))
    def _():
        tile = grad_own.shape[0]
        start = pl.multiple_of((step - 2) * tile, tile)
        dot = 0.0
        for out, index in ((grad_own, core), (grad_other, 1 - core)):
            made = tn(h[...], d_proj[index])
            out[:, : 3 * width] = made.astype(BF16)
            weight = w_in[:, index].reshape(made.shape).astype(F32)
            dot = dot + jnp.sum(made * weight, -1, keepdims=True)
            out[:, 3 * width :] = tn(full[:, pl.ds(start, tile)], mixed[index]).astype(BF16)
        gain_dots[...] = jnp.broadcast_to(dot, gain_dots.shape)

    @pl.when(step >= 2 + tiles)
    def _():
        sent[...] = back_tile(d_proj, w_in, tokens, inverse, dots, gain, full.shape[1]).astype(BF16)


def mixer_back(
    scalars, own, arrived, weights, proj, edge, later, taps, h, mixed, tokens, inverse, gain
):
    half, features = own.shape
    rows = 2 * half
    blocks, _, chunk, _ = weights.shape
    width = proj.shape[2] // 3
    tile = 256

    def per_core(shape):
        return pl.BlockSpec((1, *shape), lambda t, s: (jnp.minimum(t, 1), 0, 0))

    def whole(shape):
        return pl.BlockSpec(shape, lambda t, s: (0,) * len(shape))

    tiles = features // tile

    def tiled(block):
        return pl.BlockSpec(
            block, lambda t, s: (jnp.clip(t - 2, 0, tiles - 1),) + (0,) * (len(block) - 1)
        )

    def back(t, s):
        return (1 - s[1]) * (tiles // 2) + jnp.maximum(t - 2 - tiles, 0)

    def of_tile(t, s):
        return jnp.where(t < 2 + tiles, jnp.maximum(t - 2, 0), back(t, s))

    return pl.pallas_call(
        mixer_back_kernel,
        out_shape=[
            jax.ShapeDtypeStruct((rows, features), BF16),
            jax.ShapeDtypeStruct((2, rows, 3 * width), BF16),
            jax.ShapeDtypeStruct((2, rows, 1), F32),
            jax.ShapeDtypeStruct((2, 8, width), F32),
            jax.ShapeDtypeStruct((features, 4 * width), BF16),
            jax.ShapeDtypeStruct((features, 4 * width), BF16),
            jax.ShapeDtypeStruct((features, 128), F32),
            jax.ShapeDtypeStruct((rows, features // 2), BF16),
        ],
        grid_spec=pltpu.PrefetchScalarGridSpec(
            num_scalar_prefetch=1,
            grid=(2 + tiles + tiles // 2,),
            in_specs=[
                whole((half, features)),
                whole((half, features)),
                pl.BlockSpec((blocks, 1, chunk, width), lambda t, s: (0, jnp.minimum(t, 1), 0, 3)),
                per_core((rows, 3 * width)),
                per_core((2, width)),
                per_core((2, width)),
                per_core((3, width)),
                pl.BlockSpec((rows, tile), lambda t, s: (0, jnp.clip(t - 2, 0, tiles - 1))),
                whole((2, rows, width)),
                pl.BlockSpec(
                    (tile // chunk, 2, chunk, 3 * width), lambda t, s: (of_tile(t, s), 0, 0, 0)
                ),
                pl.BlockSpec((rows, tile), lambda t, s: (0, back(t, s))),
                whole((rows, 1)),
                pl.BlockSpec((1, tile), lambda t, s: (0, back(t, s))),
            ],
            out_specs=[
                whole((rows, features)),
                whole((2, rows, 3 * width)),
                whole((2, rows, 1)),
                per_core((8, width)),
                tiled((tile, 4 * width)),
                tiled((tile, 4 * width)),
                tiled((tile, 128)),
                pl.BlockSpec((rows, tile), lambda t, s: (0, jnp.maximum(t - 2 - tiles, 0))),
            ],
        ),
        compiler_params=pltpu.CompilerParams(vmem_limit_bytes=VMEM_LIMIT),
        name="mixer_back",
    )(
        scalars, own, arrived, weights, proj, edge, later, taps, h, mixed, weights, tokens, inverse, gain
    )


def body(
    tokens,
    in_weight,
    conv_kernel,
    out_weight,
    gate_weight,
    up_weight,
    down_weight,
    mixer_norm_gain,
    gain_ffn,
    cotangent,
):
    x, z, y, c = (lax.axis_index(name) for name in ("dp", "tok", "y", "c"))
    nx, nz = lax.axis_size("dp"), lax.axis_size("tok")
    width = tokens.shape[1]
    features = 4 * width
    rows = tokens.shape[0] // 2
    half = rows // 2
    chunk = in_weight.shape[0]
    pair = 2 * width
    scalars = jnp.stack([c, y, x])
    gain_row = mixer_norm_gain[None]

    def to_mp(value):
        mine, theirs = pick_rows(value, c, rows), pick_rows(value, 1 - c, rows)
        cross = [(2 * i + j, 2 * (1 - i) + 1 - j) for i in (0, 1) for j in (0, 1)]
        return mine, swap(theirs, "c"), swap(mine, "y"), lax.ppermute(theirs, ("y", "c"), cross)

    def join_mp(mine, beside, across, cross):
        near = by_rank(c, mine, beside, 1)
        return near, by_rank(y, near, by_rank(c, across, cross, 1), 1)

    every = ("dp", "tok", "c")

    def gather(shard):
        shard = with_layout_constraint(shard, Layout((0, 1)))
        whole = lax.all_gather(shard, every, axis=0, tiled=True)
        return whole.reshape(features // chunk, 2, chunk, shard.shape[1])

    first = jnp.concatenate([in_weight.reshape(chunk, 3 * width), out_weight.T], 1)
    first = with_layout_constraint(first, Layout((0, 1)))
    blocks = [first] + [fetch(first, "tok", i) for i in range(1, nz)]
    weights = jnp.concatenate([gate_weight, up_weight, down_weight.T], 1)
    pieces = to_mp(tokens)
    weights, cotangent, *pieces = tie(weights, cotangent, *pieces, *blocks)
    pieces, blocks = pieces[:-nz], pieces[-nz:]
    weights = gather(weights)
    first_tok = lax.dynamic_slice_in_dim(
        jnp.concatenate(blocks + blocks[:-1], 0), ((nz - z) % nz) * chunk, nz * chunk
    )
    pieces_cot = to_mp(cotangent)
    taps = by_rank(c, conv_kernel[None], swap(conv_kernel, "c")[None]).astype(F32)

    def both_cores(part):
        mine, theirs = (v.reshape(-1, 1, chunk, v.shape[1]) for v in (part, swap(part, "c")))
        return by_rank(c, mine, theirs, 1)

    if nx == 2:
        first_dp = swap(first_tok, "dp")
        first_tok = both_cores(first_tok)
    else:
        first = lax.all_gather(both_cores(first_tok), "dp", axis=0, tiled=True)

    _, full = join_mp(*pieces)
    h_mix, inverse_mix = run_jobs("norm", scalars, [norm_job(full, gain_row)], 12)
    if nx == 2:
        first_dp, first_tok, h_mix, *pieces_cot = tie(first_dp, first_tok, h_mix, *pieces_cot)
        first = by_rank(x, first_tok, both_cores(first_dp))
    _, cot = join_mp(*pieces_cot)
    cot = jnp.concatenate([pick_rows(cot, y, half), pick_rows(cot, 1 - y, half)], 0)
    cot, cot_beside = tie(cot, swap(cot, "c"))

    ranks = nz * 2
    [gated] = run_jobs("tail", scalars, [tail_job(h_mix, first, width)], 16)
    edge = lax.ppermute(gated[:, -2:], ("tok", "c"), [(i, i + 1) for i in range(ranks - 1)])
    [proj] = run_jobs("project", scalars, [project_job(h_mix, first, width)], 20)
    gate_c = proj[:, :8, width : 2 * width]
    edge, proj = tie(edge, proj)
    mixed_in, sent = run_jobs("mix", scalars, [mix_job(proj, edge, taps, first)], 28)

    def own_rows(s):
        return s[1]

    def other_rows(s):
        return 1 - s[1]

    arrived = swap(sent, "y")
    [kept] = run_jobs(
        "project_out", scalars, [back_job((mixed_in,), first, (3,), own_rows, F32)], 20
    )
    w_out = [first[:, i, :, 3 * width :].reshape(features, width) for i in (0, 1)]
    arrived, kept, *w_out = tie(arrived, kept, *w_out)
    residual = pick_rows(full, y, half).astype(F32) + kept + arrived.astype(F32)

    inverse_ffn = lax.rsqrt(jnp.mean(residual * residual, -1, keepdims=True) + EPS)
    normalized = residual * inverse_ffn
    h_own = (normalized * gain_ffn).astype(BF16)
    h, *units = hidden_units(scalars, h_own, swap(h_own, "y"), cot, weights)
    hidden, d_gate, d_up = units[:2], units[2:4], units[4:]

    def of_core(other):
        return swap(other, "c")

    def pieces_of(send):
        size = features // nx
        return to_dp([send[i * size : (i + 1) * size] for i in range(nx - 1)])

    hidden_beside, h_beside = of_core(hidden[1]), of_core(h)
    [sent] = run_jobs(
        "back_hidden", scalars, [hidden_back_job([*d_gate, *d_up], weights, (0, 1), 1)]
    )
    sent, hidden_beside, h_beside, *units = tie(sent, hidden_beside, h_beside, *hidden, *d_gate, *d_up)
    hidden, d_gate, d_up = units[:2], units[2:4], units[4:]
    gate_beside, up_beside = of_core(d_gate[1]), of_core(d_up[1])
    keep, send = run_jobs(
        "down_gradient",
        scalars,
        [gradient_job([cot, cot_beside], [hidden[0], hidden_beside], nx)],
    )
    sent, keep, send, gate_beside, up_beside, *units = tie(
        sent, keep, send, gate_beside, up_beside, *hidden, *d_gate, *d_up
    )
    hidden, d_gate, d_up = units[:2], units[2:4], units[4:]
    arrived, pieces = swap(sent, "y"), pieces_of(send)
    next_keep, send, kept = run_jobs(
        "gate_gradient",
        scalars,
        [
            gradient_job([h, h_beside], [d_gate[0], gate_beside], nx),
            hidden_back_job([*d_gate, *d_up], weights, (0, 1), 0),
        ],
    )
    arrived, send, kept, *pieces = tie(arrived, send, kept, *pieces)
    d_h = kept.astype(F32) + arrived.astype(F32)
    grad_gain_ffn = jnp.sum(d_h * normalized, 0)
    scaled = d_h * gain_ffn
    d_res = cot[:half].astype(F32) + inverse_ffn * (
        scaled - normalized * jnp.mean(scaled * normalized, -1, keepdims=True)
    )
    d_res_own = d_res.astype(BF16)
    down_parts = [keep, *pieces]
    down_mine = [for_tok(down_parts, i).astype(BF16) for i in range(1, nz)]
    d_res_own, send, *units = tie(d_res_own, send, *hidden, *d_up, *down_mine)
    hidden, d_up, down_mine = units[:2], units[2:4], units[4:]
    arrived, pieces = swap(d_res_own, "y"), pieces_of(send)
    down_got = [deliver(part, "tok", i + 1) for i, part in enumerate(down_mine)]
    keep, send, made_sent, made_kept = run_jobs(
        "up_gradient",
        scalars,
        [
            gradient_job([h, h_beside], [d_up[0], up_beside], nx),
            made_job(hidden, weights, 2, residual),
        ],
    )
    arrived, send, made_sent, made_kept, *pieces = tie(
        arrived, send, made_sent, made_kept, *pieces, *down_got
    )
    pieces, down_got = pieces[: 1 - nz], pieces[1 - nz :]
    grad_down = total([for_tok(down_parts, 0), *down_got])
    gate_parts = [next_keep, *pieces]
    gate_mine = [for_tok(gate_parts, i).astype(BF16) for i in range(1, nz)]

    head = jnp.where(y == 0, d_res_own[:8], arrived[:8])
    d_head = jnp.stack([nn(head, w) for w in w_out])
    d_head = (d_head * gate_c).astype(BF16)[:, :2]
    later = lax.ppermute(d_head, ("tok", "c"), [(i + 1, i) for i in range(ranks - 1)])
    arrived, later, send, *gate_mine = tie(arrived, later, send, *gate_mine)
    pieces = pieces_of(send)
    gate_got = [deliver(part, "tok", i + 1) for i, part in enumerate(gate_mine)]
    d_res_full, d_proj, dots, grad_taps, own, other, gain_dots, sent = mixer_back(
        scalars,
        d_res_own,
        arrived,
        first,
        proj,
        edge,
        later,
        taps,
        h_mix,
        mixed_in,
        full,
        inverse_mix,
        gain_row,
    )
    d_proj, own, other, sent, *pieces = tie(d_proj, own, other, sent, *pieces, *gate_got)
    pieces, gate_got = pieces[: 1 - nz], pieces[1 - nz :]
    grad_gate = total([for_tok(gate_parts, 0), *gate_got])
    other = of_core(other)
    up_mine = add_dp(keep, pieces)
    sent, d_proj, up_mine, grad_taps, gain_dots, own, other, *pieces = tie(
        sent, d_proj, up_mine, grad_taps, gain_dots, own, other, *for_dp(own, other)
    )
    arrived, up_got, pieces = swap(sent, "y"), to_tok(up_mine), to_dp(pieces)
    near_sums = jnp.concatenate([grad_taps[0, :3], grad_taps[1, :3]], 1)
    sums = lax.dynamic_update_slice(jnp.zeros((3, features), F32), near_sums, (0, y * pair))
    gain_sum = gain_dots[:, 0] / mixer_norm_gain
    sums = jnp.concatenate([sums, gain_sum[None], grad_gain_ffn[None]], 0)
    sums = sum_over(sums, "c")
    if nx == 2:
        cross = [(2 * i + j, 2 * (1 - i) + 1 - j) for i in (0, 1) for j in (0, 1)]
        near, far = swap(sums, "y"), lax.ppermute(sums, ("dp", "y"), cross)
        sums = [sums, near, swap(sums, "dp"), far]
    else:
        sums = [sum_over(sum_over(sums, "dp"), "y")]
    [kept] = run_jobs(
        "back_in",
        scalars,
        [back_in_job(d_proj, first, full, inverse_mix, dots, gain_row, own_rows, F32)],
    )
    arrived, kept, up_got, sums, keep, *pieces = tie(
        arrived, kept, up_got, sums, for_self(own, other), *pieces
    )
    sums = (sums[0] + sums[1]) + (sums[2] + sums[3]) if nx == 2 else sums[0]
    mixer_parts = [keep, *pieces]

    high = sums.astype(BF16)
    low = (sums - high.astype(F32)).astype(BF16)
    extra = jnp.concatenate([high, low, jnp.zeros((16 - 2 * sums.shape[0], features), BF16)], 0)
    extra_own = jnp.concatenate([jnp.zeros((chunk, features), BF16), extra], 0)
    mixer_mine = [
        jnp.concatenate([for_tok(mixer_parts, i).astype(BF16), extra], 0) for i in range(1, nz)
    ]
    arrived, *mixer_mine = tie(arrived, *mixer_mine)
    mixer_got = [deliver(part, "tok", i + 1) for i, part in enumerate(mixer_mine)]
    made_sent, arrived = tie(made_sent, arrived)
    made_arrived = swap(made_sent, "y")

    d_res_near = jnp.where(y == 0, d_res_full[:, :pair], d_res_full[:, pair:]).astype(F32)

    def by_core(value):
        mine = jnp.where(c == 0, value[:, :width], value[:, width:])
        theirs = jnp.where(c == 0, value[:, width:], value[:, :width])
        return by_rank(c, mine, swap(theirs, "c"))

    input_gradient = by_core(
        d_res_near + inverse_mix * (kept + arrived.astype(F32))
    )
    out_near = by_rank(
        y,
        (made_kept[:half] + made_arrived[half:].astype(F32)).astype(BF16),
        (made_kept[half:] + made_arrived[:half].astype(F32)).astype(BF16),
    )
    mixed = by_core(out_near)
    grad_up = add_tok(up_got)
    mixed, input_gradient, *mixer_got = tie(mixed, input_gradient, *mixer_got)
    grad_mixer = total([for_tok(mixer_parts, 0), *[part[:chunk] for part in mixer_got]])
    sums = [part[chunk : chunk + 10].astype(F32) for part in (extra_own, *mixer_got)]
    if nz == 4:
        sums = (sums[0] + sums[2]) + (sums[1] + sums[3])
    else:
        by_tok = jnp.stack(sums)
        sums = sum(
            (lax.dynamic_index_in_dim(by_tok, (z - i) % nz, 0, False) for i in range(nz)),
            jnp.zeros_like(sums[0]),
        )
    sums = sums[:5] + sums[5:]
    grad_in = grad_mixer[:, : 3 * width].reshape(chunk, 3, width)
    grad_out = grad_mixer[:, 3 * width :].T

    sums = lax.dynamic_slice_in_dim(sums, (2 * y + c) * width, width, 1)

    return (
        mixed,
        input_gradient,
        grad_in,
        sums[:3],
        grad_out,
        grad_gate,
        grad_up,
        grad_down.T,
        sums[3],
        sums[4],
    )


def solution(mesh):
    split = Mesh(
        mesh.devices.reshape(mesh.shape["dp"], mesh.shape["tok"], mesh.shape["mp"] // 2, 2),
        ("dp", "tok", "y", "c"),
    )
    tok, mp = ("dp", "tok"), ("y", "c")
    return jax.shard_map(
        body,
        mesh=split,
        in_specs=(
            P(tok, mp),
            P(tok, None, mp),
            P(None, mp),
            P(mp, tok),
            P(tok, mp),
            P(tok, mp),
            P(mp, tok),
            P(),
            P(),
            P(tok, mp),
        ),
        out_specs=(
            P(tok, mp),
            P(tok, mp),
            P(tok, None, mp),
            P(None, mp),
            P(mp, tok),
            P(tok, mp),
            P(tok, mp),
            P(mp, tok),
            P(mp),
            P(mp),
        ),
        check_vma=False,
    )
```
